32 devices in a mesh: member: 2 (over x), gx: 4 (over z), gy: 4 (over y, core).
Axes of the slice: x: 2, y: 2, z: 4, core: 2. Of those that a mesh axis runs over, the one named last changes fastest.
Arguments:
- perturb: bfloat16 [4, 20, 192, 512], P('member', None, 'gx', 'gy'), may hold values from -6 to 6
- gradient: float32 [20, 192, 512], P(None, 'gx', 'gy'), may hold values from -6 to 6
- vertical_eigenmodes: float32 [20, 20], replicated, may hold values from -1.25 to 1.25
- rate_x: float32 [20], replicated, may hold values from 1 to 512, as said below
- rate_y: float32 [20], replicated, may hold values from 1 to 512, as said below
Outputs:
- increment: float32 [20, 192, 512], P(None, 'gx', 'gy')
The draws below stay inside these ranges and needn't reach their ends.
Inputs may be any that keep to these rules, and one draw needn't show every extreme that they name: `rate_x`: one rate for each mode. `rate_y`: one rate for each mode.
All inputs are finite; a program needn't handle non-finite values.
Results may differ from the reference program's by a relative error of at most 0.0003.
Values sent between devices are 32-bit elements; how exact they have to be, the bound alone decides.
No kernel may reach another device: no remote copies, remote signals or barrier semaphores. Data moves between devices by JAX's collectives and lax.ppermute only.
A program may use at most 64 MiB of HBM per device.

```python
import math
import jax
import jax.numpy as jnp
from jax import lax

LEV = 20
MODES = 20
MEMBERS = 4
NX = 192
NY = 512


def mode_rates(key, salt):
    base = jax.random.fold_in(key, salt)
    key_order, key_slow, key_fast = jax.random.split(base, 3)
    order = jax.random.permutation(key_order, MODES)
    slow_count = MODES // 2
    slow_mask = order < slow_count
    slow_rates = jnp.exp(jax.random.uniform(key_slow, (MODES,), jnp.float32, math.log(1.0), math.log(2.0)))
    fast_rates = jnp.exp(jax.random.uniform(key_fast, (MODES,), jnp.float32, math.log(16.0), math.log(512.0)))
    return jnp.where(slow_mask, slow_rates, fast_rates).astype(jnp.float32)


def draw_rate_x(key, part):
    return mode_rates(key, 11)


def draw_rate_y(key, part):
    return mode_rates(key, 23)


def level_of(stream_key, shape, shards, least, largest):
    def one(dim, parts):
        steps = jax.random.uniform(jax.random.fold_in(jax.random.fold_in(stream_key, 6), dim), (parts,), jnp.float32, least / len(shards), largest / len(shards))
        return jnp.repeat(jnp.exp(steps), shape[dim] // parts).reshape((-1,) + (1,) * (len(shape) - dim - 1))

    gain = one(*shards[0])
    for cut in shards[1:]:
        gain = gain * one(*cut)
    return gain


def bell_draw(rng, shape, width, most, cuts=(), dtype=jnp.bfloat16):
    array = jax.random.normal(rng, shape, jnp.float32) * width
    if len(cuts) > 0:
        array = level_of(rng, shape, cuts, -0.22, 0.18) * array
    return jnp.clip(array, min=-most, max=most).astype(dtype)


def setup_inputs(seed: int = 0) -> dict:
    key_list = jax.random.split(jax.random.key(seed), 6)
    return {
        "perturb": bell_draw(key_list[0], (MEMBERS, LEV, NX, NY), 1.0, 6.0, ((0, 2), (2, 4), (3, 4))),
        "gradient": bell_draw(key_list[1], (LEV, NX, NY), 1.0, 6.0, ((1, 4), (2, 4)), jnp.float32),
        "vertical_eigenmodes": bell_draw(key_list[2], (LEV, MODES), LEV ** -0.5, 1.25, (), jnp.float32),
        "rate_x": draw_rate_x(jax.random.fold_in(key_list[5], 71), 0),
        "rate_y": draw_rate_y(jax.random.fold_in(key_list[5], 71), 0),
    }


def cascade(shrink, amplification, inputs, initial):

    def advance_one(states, ensemble_sample):
        section_one = shrink * states[0] + amplification * ensemble_sample
        section_two = shrink * states[1] + amplification * section_one
        section_three = shrink * states[2] + amplification * section_two
        section_four = shrink * states[3] + amplification * section_three
        return (jnp.stack([section_one, section_two, section_three, section_four]), section_four)
    finals, outputs = lax.scan(advance_one, initial, inputs)
    return (outputs, finals)

def line_filter(values, decay_rate, extent):
    shrink = jnp.exp(-decay_rate / extent)[:, None]
    amplification = -jnp.expm1(-decay_rate / extent)[:, None]
    starting = jnp.zeros((4,) + values.shape[1:], jnp.float32)
    onward, _ = cascade(shrink, amplification, values, starting)
    returned, _ = cascade(shrink, amplification, onward[::-1], starting)
    factor = jnp.sqrt((2.0 - amplification) / amplification)
    return returned[::-1] * factor

def reference(perturb, gradient, vertical_eigenmodes, rate_x, rate_y):
    extent_x = gradient.shape[1]
    extent_y = gradient.shape[2]

    def member_step(running, member_rows):
        weights = member_rows.astype(jnp.float32)
        projected = jnp.einsum('lm,lxy->xmy', vertical_eigenmodes, weights * gradient, precision=lax.Precision.HIGHEST)
        projected = line_filter(projected, rate_x, extent_x)
        rotated_field = jnp.transpose(projected, (2, 1, 0))
        rotated_field = line_filter(rotated_field, rate_y, extent_y)
        recovered_field = jnp.einsum('hz,dzo->hod', vertical_eigenmodes, rotated_field, precision=lax.Precision.HIGHEST)
        return (running + weights * recovered_field, None)
    running, _ = lax.scan(member_step, jnp.zeros(gradient.shape, jnp.float32), perturb)
    return running / (perturb.shape[0] - 1)
```

```python
import functools

import jax
import jax.numpy as jnp
from jax import lax
from jax.experimental import pallas as pl
from jax.experimental.pallas import tpu as pltpu
from jax.sharding import PartitionSpec as P

F32 = jnp.float32
BF16 = jnp.bfloat16
VMEM = pltpu.VMEM
SMEM = pltpu.SMEM
ORDER = 4
LANES = 128
SUB = 8


def poly(d, n):
    if d == 0:
        return jnp.ones_like(n) if hasattr(n, "shape") else 1.0
    if d == 1:
        return n
    if d == 2:
        return n * (n + 1.0) * 0.5
    return n * (n + 1.0) * (n + 2.0) * (1.0 / 6.0)


def gain(z):
    series = jnp.ones_like(z)
    for k in range(12, 1, -1):
        series = 1.0 - z * series * (1.0 / k)
    return jnp.where(z < 1.0, z * series, 1.0 - jnp.exp(-z))


def split(a):
    high = a.astype(BF16)
    return high, (a - high.astype(F32)).astype(BF16)


def dot(a, b):
    return jnp.dot(a, b, preferred_element_type=F32)


def dot3(a, b):
    return dot(a[0], b[0]) + (dot(a[0], b[1]) + dot(a[1], b[0]))


def exact(a, b, contract=((1,), (0,))):
    return lax.dot_general(
        a, b, (contract, ((), ())), precision=lax.Precision.HIGHEST, preferred_element_type=F32
    )


def iota(shape, axis):
    return lax.broadcasted_iota(jnp.int32, shape, axis)


def column_of(row, pick, rows):
    n = row.shape[1]
    wide = jnp.broadcast_to(row, (rows, n))
    hit = iota((rows, n), 1) == pick(iota((rows, n), 0))
    return jnp.sum(jnp.where(hit, wide, 0.0), axis=1, keepdims=True)


def expanded(matrix, rows, cols):
    left = (iota((rows * SUB, rows), 0) // SUB == iota((rows * SUB, rows), 1)).astype(F32)
    right = (iota((cols, cols * SUB), 1) // SUB == iota((cols, cols * SUB), 0)).astype(F32)
    full = exact(exact(left, matrix), right)
    shape = (rows * SUB, cols * SUB)
    return jnp.where(iota(shape, 0) % SUB == iota(shape, 1) % SUB, full, 0.0)


def shifted(coefficients, states):
    out = []
    for a in range(ORDER):
        total = coefficients[0] * states[a]
        for c in range(a):
            total = total + coefficients[a - c] * states[c]
        out.append(total)
    return out


def power(z, steps):
    decay = jnp.exp(-z * float(steps))
    return [decay * poly(d, float(steps)) for d in range(ORDER)]


def section(r, states, value):
    out = []
    for s in states:
        value = r * s + value
        out.append(value)
    return tuple(out)


def project_kernel(blocks, extent, p_ref, g_ref, e_ref, rx_ref, proj_ref, msg_ref, hat_ref, w_ref, y_ref):
    members, levels, nx, ny = p_ref.shape
    modes = e_ref.shape[1]
    rows = members * modes
    place = lax.axis_index("gx")
    rate = rx_ref[...]

    for m in range(members):
        for l in range(levels):
            w_ref[pl.ds((m * levels + l) * nx, nx), :] = p_ref[m, l].astype(F32) * g_ref[l]

    z_rows = column_of(rate, lambda i: i // SUB, modes * SUB) * (1.0 / extent)
    g_rows = gain(z_rows)
    mix = split(expanded(e_ref[...].T, modes, levels) * (g_rows * g_rows) * (g_rows * g_rows))
    for t in range(nx // SUB):
        wide = jnp.concatenate(
            [
                jnp.concatenate(
                    [w_ref[pl.ds((m * levels + l) * nx + t * SUB, SUB), :] for l in range(levels)], 0
                )
                for m in range(members)
            ],
            1,
        )
        done = dot3(mix, split(wide))
        for m in range(members):
            for k in range(modes):
                proj_ref[pl.ds((m * modes + k) * nx + t * SUB, SUB), :] = done[
                    k * SUB : (k + 1) * SUB, m * ny : (m + 1) * ny
                ]

    z = column_of(rate, lambda i: i % modes, rows) * (1.0 / extent)
    g = gain(z)
    full = (rows, ny)
    r = jnp.broadcast_to(jnp.exp(-z), full)
    pass_gain = jnp.broadcast_to((g * g) * (g * g), full)
    zeros = (jnp.zeros(full, F32),) * ORDER

    def onward(x, states):
        states = section(r, states, proj_ref[pl.ds(x, rows, stride=nx), :])
        y_ref[pl.ds(pl.multiple_of(x * rows, SUB), rows), :] = states[-1] * pass_gain
        return states

    def backward(n, states):
        x = nx - 1 - n
        return section(r, states, y_ref[pl.ds(pl.multiple_of(x * rows, SUB), rows), :])

    ends = lax.fori_loop(0, nx, onward, zeros, unroll=8)
    starts = lax.fori_loop(0, nx, backward, zeros, unroll=8)

    ahead = (blocks - 1 - place) * nx
    span = (blocks - 1) * nx
    span = -(-span // LANES) * LANES
    n = iota((rows, span), 1).astype(F32) + 1.0
    inside = iota((rows, span), 1) < ahead
    weight = jnp.where(inside, jnp.exp(-z * (2.0 * n - 1.0)), 0.0) * ((g * g) * (g * g))
    sums = {}
    for a in range(ORDER):
        for b in range(a, ORDER):
            sums[a, b] = jnp.sum(weight * poly(a, n) * poly(b, n), axis=1, keepdims=True)
            sums[b, a] = sums[a, b]
    hat = [[sums[a, ORDER - 1 - b] for b in range(ORDER)] for a in range(ORDER)]
    lane = iota((rows, LANES), 1)
    packed = jnp.zeros((rows, LANES), F32)
    for a in range(ORDER):
        for b in range(ORDER):
            packed = jnp.where(lane == a * ORDER + b, hat[a][b], packed)
    hat_ref[...] = packed

    turned = [sum(hat[a][b] * ends[b] for b in range(ORDER)) for a in range(ORDER)]
    turned = shifted(power(z, nx), turned)
    leaving = [starts[a] + turned[a] for a in range(ORDER)]
    for d in range(1, blocks):
        to_right = ends if d == 1 else shifted(power(z, (d - 1) * nx), ends)
        hops = blocks - d
        to_left = leaving if hops == 1 else shifted(power(z, (hops - 1) * nx), leaving)
        for a in range(ORDER):
            msg_ref[d - 1, pl.ds(a * rows, rows), :] = jnp.where(
                place + d < blocks, to_right[a], to_left[a]
            )


def table_kernel(blocks, extent, extent_x, e_ref, rx_ref, ry_ref, ry_s, send_ref, dy_ref, fix_ref, lift_ref, p_ref):
    modes = e_ref.shape[1]
    ny = dy_ref.shape[1]
    place = lax.axis_index("gy")
    states = modes * ORDER

    spread = (iota((modes, LANES), 1) // ORDER == iota((modes, LANES), 0)).astype(F32)
    live = (iota((1, LANES), 1) < states).astype(F32)
    lift = exact(e_ref[...], spread)
    lift_ref[...] = jnp.concatenate([lift, lift], 1)
    z = exact(ry_ref[...], spread) * (1.0 / extent)
    zx = exact(rx_ref[...], spread) * (1.0 / extent_x)
    g = gain(z)
    gx = gain(zx)
    pass_gain = (g * g) * (g * g) * live
    scale = jnp.sqrt((2.0 - g) / jnp.where(live > 0, g, 1.0)) * jnp.sqrt(
        (2.0 - gx) / jnp.where(live > 0, gx, 1.0)
    )
    scale = scale * live
    square = (LANES, LANES)
    eye = iota(square, 0) == iota(square, 1)

    def to_column(row):
        return jnp.sum(jnp.where(eye, jnp.broadcast_to(row, square), 0.0), axis=1, keepdims=True)

    def pick(index, choices):
        out = choices[0]
        for k in range(1, len(choices)):
            out = jnp.where(index == k, choices[k], out)
        return out

    z_col = to_column(z)
    scale_col = to_column(scale)
    gain_col = to_column(pass_gain)
    same = iota(square, 0) // ORDER == iota(square, 1) // ORDER
    row_state = iota(square, 0) % ORDER
    lane_state = iota(square, 1) % ORDER

    def moved(steps):
        if steps == 0:
            return jnp.where(eye, 1.0, 0.0)
        decay = jnp.exp(-z * float(steps))
        up = lane_state - row_state
        by = pick(up, [poly(d, float(steps)) for d in range(ORDER)])
        return jnp.where(same & (up >= 0), decay * by, 0.0)

    ahead = (blocks - 1 - place) * ny
    span = (blocks - 1) * ny
    n = iota((LANES, span), 1).astype(F32) + 1.0
    state = iota((LANES, span), 0) % ORDER
    inside = iota((LANES, span), 1) < ahead
    polys = [poly(d, n) for d in range(ORDER)]
    first = jnp.where(inside, jnp.exp(-z_col * n), 0.0) * pick(state, polys[::-1])
    second = jnp.exp(-z_col * (n - 1.0)) * pick(state, polys)
    hat = jnp.where(same, exact(first, second, ((1,), (1,))), 0.0)

    j = iota((ny, LANES), 0).astype(F32)
    lanes = iota((ny, LANES), 1) % ORDER
    from_end = float(ny) - j
    st = jnp.exp(-z * (from_end - 1.0)) * pick(lanes, [poly(a, from_end) for a in range(ORDER)]) * live
    sbt = jnp.exp(-z * j) * pick(lanes, [poly(a, j + 1.0) for a in range(ORDER)]) * live
    c_n = float(ny) - iota((LANES, ny), 1).astype(F32)
    c_state = iota((LANES, ny), 0) % ORDER
    cbt = jnp.exp(-z_col * c_n) * pick(c_state, [poly(ORDER - 1 - a, c_n) for a in range(ORDER)])
    bent = exact(st, hat)

    gap = iota((ny, ny), 1) - iota((ny, ny), 0)
    distance = jnp.maximum(gap, 0).astype(F32)
    p_ref[...] = jnp.where(gap >= 0, poly(ORDER - 1, distance + 1.0), 0.0)
    group = iota((ny, LANES), 1) // ORDER
    seen = jnp.zeros((ny, LANES), F32)
    for k in range(modes):
        rate = ry_s[k] * (1.0 / extent)
        up = jnp.exp(distance * (-rate)) * p_ref[...]
        mine = group == k
        seen = seen + exact(up, jnp.where(mine, sbt, 0.0))
        core = exact(up, up, ((1,), (1,))) + exact(jnp.where(mine, bent, 0.0), cbt)
        total = jnp.max(jnp.where(iota((1, LANES), 1) // ORDER == k, pass_gain * pass_gain * scale, 0.0))
        dy_ref[k] = core * total

    leaving = (seen + exact(bent, moved(ny))) * (pass_gain * pass_gain)
    for d in range(1, blocks):
        ends = float(d * ny) - j
        to_right = jnp.exp(-z * (ends - 1.0)) * pick(lanes, [poly(a, ends) for a in range(ORDER)]) * pass_gain
        to_left = exact(leaving, moved((blocks - d - 1) * ny))
        send_ref[:, pl.ds((d - 1) * LANES, LANES)] = jnp.where(place + d < blocks, to_right, to_left)

    flip = same & (row_state + lane_state == ORDER - 1)
    turned = exact(jnp.where(flip, jnp.exp(-z_col), 0.0), seen, ((1,), (1,)))
    bent_on = exact(exact(moved(ny), hat), cbt)
    fix_ref[0:LANES, :] = (turned + bent_on) * (gain_col * scale_col)
    fix_ref[LANES : 2 * LANES, :] = cbt * scale_col


def x_kernel(blocks, blocks_y, extent, proj_ref, hat_ref, rx_ref, send_ref, *refs):
    got = refs[: blocks - 1]
    z_ref, msg_refs, y_ref = refs[blocks - 1], refs[blocks:-1], refs[-1]
    rows = hat_ref.shape[0]
    modes = rx_ref.shape[1]
    members = rows // modes
    ny = proj_ref.shape[1]
    nx = proj_ref.shape[0] // rows
    place = lax.axis_index("gx")
    full = (rows, ny)
    z = column_of(rx_ref[...], lambda i: i % modes, rows) * (1.0 / extent)
    g = gain(z)
    r = jnp.broadcast_to(jnp.exp(-z), full)
    pass_gain = jnp.broadcast_to((g * g) * (g * g), full)

    left, right = [], []
    for a in range(ORDER):
        e = jnp.zeros(full, F32)
        b = jnp.zeros(full, F32)
        for d in range(1, blocks):
            value = got[d - 1][pl.ds(a * rows, rows), :]
            e = e + jnp.where(place >= d, value, 0.0)
            b = b + jnp.where(place >= d, 0.0, value)
        left.append(e)
        right.append(b)

    def onward(x, states):
        states = section(r, states, proj_ref[pl.ds(x, rows, stride=nx), :])
        y_ref[pl.ds(pl.multiple_of(x * rows, SUB), rows), :] = states[-1] * pass_gain
        return states

    def backward(n, states):
        x = nx - 1 - n
        at = pl.ds(pl.multiple_of(x * rows, SUB), rows)
        states = section(r, states, y_ref[at, :])
        z_ref[at, :] = states[-1]
        return states

    ends = lax.fori_loop(0, nx, onward, tuple(left), unroll=8)
    hat = hat_ref[...]
    for a in range(ORDER):
        for b in range(ORDER):
            at = a * ORDER + b
            right[a] = right[a] + hat[:, at : at + 1] * ends[b]
    lax.fori_loop(0, nx, backward, tuple(right), unroll=8)

    send = send_ref[...]
    group = (iota(send.shape, 1) % LANES) // ORDER
    total = jnp.zeros((members * nx, send.shape[1]), F32)
    for k in range(modes):
        value = jnp.concatenate(
            [z_ref[pl.ds(m * modes + k, nx, stride=rows), :] for m in range(members)], 0
        )
        total = total + dot3(split(value), split(jnp.where(group == k, send, 0.0)))
    for d in range(blocks_y - 1):
        msg_refs[d][...] = total[:, d * LANES : (d + 1) * LANES]


def local_kernel(z_ref, dy_ref, e_ref, out_ref, f_ref):
    levels, modes = e_ref.shape
    members = out_ref.shape[0] // levels
    nx = out_ref.shape[1]
    ny = z_ref.shape[1]
    rows = members * modes
    for k in range(modes):
        value = jnp.concatenate(
            [z_ref[pl.ds(m * modes + k, nx, stride=rows), :] for m in range(members)], 0
        )
        done = dot3(split(value), split(dy_ref[k]))
        for m in range(members):
            f_ref[pl.ds((m * modes + k) * nx, nx), :] = done[m * nx : (m + 1) * nx]
    mix = split(expanded(e_ref[...], levels, modes))
    for t in range(nx // SUB):
        wide = jnp.concatenate(
            [
                jnp.concatenate(
                    [f_ref[pl.ds((m * modes + k) * nx + t * SUB, SUB), :] for k in range(modes)], 0
                )
                for m in range(members)
            ],
            1,
        )
        done = dot3(mix, split(wide))
        for m in range(members):
            for l in range(levels):
                out_ref[m * levels + l, pl.ds(t * SUB, SUB), :] = done[
                    l * SUB : (l + 1) * SUB, m * ny : (m + 1) * ny
                ]


def final_kernel(blocks, total_members, p_ref, base_ref, fix_ref, lift_ref, *refs):
    got, out_ref = refs[:-1], refs[-1]
    members, levels, nx, ny = p_ref.shape
    place = lax.axis_index("gy")
    left = jnp.zeros(got[0].shape, F32)
    right = jnp.zeros(got[0].shape, F32)
    for d in range(1, blocks):
        value = got[d - 1][...]
        left = left + jnp.where(place >= d, value, 0.0)
        right = right + jnp.where(place >= d, 0.0, value)
    enter = jnp.concatenate([left, right], 1)
    fix = split(fix_ref[...])
    share = 1.0 / (total_members - 1)
    for l in range(levels):
        add = dot3(split(enter * lift_ref[pl.ds(l, 1), :]), fix)
        out = jnp.zeros((nx, ny), F32)
        for m in range(members):
            out = out + p_ref[m, l].astype(F32) * (
                base_ref[m * levels + l] + add[m * nx : (m + 1) * nx]
            )
        out_ref[l] = out * share


def call(kernel, out, ins, scratch=(), smem=(), flops=0, name=None):
    spec = lambda i: pl.BlockSpec(memory_space=SMEM if i in smem else VMEM)
    nbytes = sum(a.size * a.dtype.itemsize for a in ins) + sum(
        a.size * a.dtype.itemsize for a in jax.tree.leaves(out)
    )
    return pl.pallas_call(
        kernel,
        out_shape=out,
        in_specs=[spec(i) for i in range(len(ins))],
        out_specs=jax.tree.map(lambda _: pl.BlockSpec(memory_space=VMEM), out),
        scratch_shapes=list(scratch),
        cost_estimate=pl.CostEstimate(flops=flops, bytes_accessed=nbytes, transcendentals=0),
        name=name,
    )(*ins)


def shape(*dims):
    return jax.ShapeDtypeStruct(dims, F32)


def turn(value, axis, distance):
    n = lax.axis_size(axis)
    return lax.ppermute(value, axis, [(i, (i + distance) % n) for i in range(n)])


def body(perturb, gradient, vertical_eigenmodes, rate_x, rate_y):
    members, levels, nx, ny = perturb.shape
    modes = vertical_eigenmodes.shape[1]
    rows = members * modes
    blocks_x, blocks_y = lax.axis_size("gx"), lax.axis_size("gy")
    extent_x, extent_y = nx * blocks_x, ny * blocks_y
    row_x, row_y = rate_x[None, :], rate_y[None, :]

    proj, messages, hat = call(
        functools.partial(project_kernel, blocks_x, extent_x),
        (shape(rows * nx, ny), shape(blocks_x - 1, ORDER * rows, ny), shape(rows, LANES)),
        (perturb, gradient, vertical_eigenmodes, row_x),
        scratch=(VMEM((members * levels * nx, ny), F32), VMEM((rows * nx, ny), F32)),
        flops=1 << 28,
        name="project",
    )
    got = [turn(messages[d - 1], "gx", d) for d in range(1, blocks_x)]
    send, local, fix, lift = call(
        functools.partial(table_kernel, blocks_y, extent_y, extent_x),
        (
            shape(ny, (blocks_y - 1) * LANES),
            shape(modes, ny, ny),
            shape(2 * LANES, ny),
            shape(levels, 2 * LANES),
        ),
        (vertical_eigenmodes, row_x, row_y, rate_y),
        scratch=(VMEM((ny, ny), F32),),
        smem=(3,),
        flops=1 << 30,
        name="tables",
    )
    outs = call(
        functools.partial(x_kernel, blocks_x, blocks_y, extent_x),
        tuple([shape(rows * nx, ny)] + [shape(members * nx, LANES)] * (blocks_y - 1)),
        (proj, hat, row_x, send, *got),
        scratch=(VMEM((rows * nx, ny), F32),),
        flops=1 << 28,
        name="along_x",
    )
    filtered, sent = outs[0], outs[1:]
    got = [turn(sent[d - 1], "gy", d) for d in range(1, blocks_y)]
    base = call(
        local_kernel,
        shape(members * levels, nx, ny),
        (filtered, local, vertical_eigenmodes),
        scratch=(VMEM((rows * nx, ny), F32),),
        flops=1 << 29,
        name="along_y",
    )
    partial = call(
        functools.partial(final_kernel, blocks_y, members * lax.axis_size("member")),
        shape(levels, nx, ny),
        (perturb, base, fix, lift, *got),
        flops=1 << 28,
        name="restore",
    )
    if lax.axis_size("member") == 2:
        return partial + turn(partial, "member", 1)
    return lax.psum(partial, "member")


def solution(mesh):
    return jax.shard_map(
        body,
        mesh=mesh,
        in_specs=(P("member", None, "gx", "gy"), P(None, "gx", "gy"), P(), P(), P()),
        out_specs=P(None, "gx", "gy"),
        check_vma=False,
    )
```

```python
import functools

import jax
import jax.numpy as jnp
from jax import lax
from jax.experimental import pallas as pl
from jax.experimental.pallas import tpu as pltpu
from jax.sharding import PartitionSpec as P

F32 = jnp.float32
BF16 = jnp.bfloat16
VMEM = pltpu.VMEM
ORDER = 4
LANES = 128
SUB = 8
GRANT = 12 << 20


def poly(d, n):
    if d == 0:
        return jnp.ones_like(n) if hasattr(n, "shape") else 1.0
    if d == 1:
        return n
    if d == 2:
        return n * (n + 1.0) * 0.5
    return n * (n + 1.0) * (n + 2.0) * (1.0 / 6.0)


def gain(z):
    series = jnp.ones_like(z)
    for k in range(12, 1, -1):
        series = 1.0 - z * series * (1.0 / k)
    return jnp.where(z < 1.0, z * series, 1.0 - jnp.exp(-z))


def split(a):
    high = a.astype(BF16)
    return high, (a - high.astype(F32)).astype(BF16)


def dot(a, b):
    return jnp.dot(a, b, preferred_element_type=F32)


def dot3(a, b):
    return dot(a[0], b[0]) + (dot(a[0], b[1]) + dot(a[1], b[0]))


def exact(a, b, contract=((1,), (0,))):
    return lax.dot_general(
        a, b, (contract, ((), ())), precision=lax.Precision.HIGHEST, preferred_element_type=F32
    )


def iota(shape, axis):
    return lax.broadcasted_iota(jnp.int32, shape, axis)


def column_of(row, pick, rows):
    n = row.shape[1]
    wide = jnp.broadcast_to(row, (rows, n))
    hit = iota((rows, n), 1) == pick(iota((rows, n), 0))
    return jnp.sum(jnp.where(hit, wide, 0.0), axis=1, keepdims=True)


def expanded(matrix, rows, cols):
    left = (iota((rows * SUB, rows), 0) // SUB == iota((rows * SUB, rows), 1)).astype(F32)
    right = (iota((cols, cols * SUB), 1) // SUB == iota((cols, cols * SUB), 0)).astype(F32)
    full = exact(exact(left, matrix), right)
    shape = (rows * SUB, cols * SUB)
    return jnp.where(iota(shape, 0) % SUB == iota(shape, 1) % SUB, full, 0.0)


def shifted(coefficients, states):
    out = []
    for a in range(ORDER):
        total = coefficients[0] * states[a]
        for c in range(a):
            total = total + coefficients[a - c] * states[c]
        out.append(total)
    return out


def power(z, steps):
    decay = jnp.exp(-z * float(steps))
    return [decay * poly(d, float(steps)) for d in range(ORDER)]


def section(r, states, value):
    out = []
    for s in states:
        value = r * s + value
        out.append(value)
    return tuple(out)


def project_kernel(blocks, extent, p_hbm, g_hbm, e_hbm, rx_hbm, ry_hbm, proj_ref, hat_ref, e_ref, rx_ref, ry_ref, *refs):
    msg_refs = refs[: blocks - 1]
    p_ref, g_ref, w_ref, n_ref, y_ref, sems = refs[blocks - 1 :]
    members, levels, nx, ny = p_ref.shape
    modes = e_ref.shape[1]
    rows = members * modes
    place = lax.axis_index("gx")
    pairs = [(e_hbm, e_ref), (rx_hbm, rx_ref), (ry_hbm, ry_ref), (g_hbm, g_ref)]
    pairs = pairs + [(p_hbm.at[m], p_ref.at[m]) for m in range(members)]
    copies = [pltpu.make_async_copy(a, b, sems.at[i]) for i, (a, b) in enumerate(pairs)]
    for copy in copies:
        copy.start()
    for copy in copies[:3]:
        copy.wait()
    rate = rx_ref[...]

    z_rows = column_of(rate, lambda i: i // SUB, modes * SUB) * (1.0 / extent)
    g_rows = gain(z_rows)
    mix = split(expanded(e_ref[...].T, modes, levels) * (g_rows * g_rows) * (g_rows * g_rows))
    for copy in copies[3:]:
        copy.wait()
    for m in range(members):
        for l in range(levels):
            w_ref[pl.ds((m * levels + l) * nx, nx), :] = p_ref[m, l].astype(F32) * g_ref[l]

    for t in range(nx // SUB):
        wide = jnp.concatenate(
            [
                jnp.concatenate(
                    [w_ref[pl.ds((m * levels + l) * nx + t * SUB, SUB), :] for l in range(levels)], 0
                )
                for m in range(members)
            ],
            1,
        )
        done = dot3(mix, split(wide))
        for m in range(members):
            for k in range(modes):
                n_ref[pl.ds((m * modes + k) * nx + t * SUB, SUB), :] = done[
                    k * SUB : (k + 1) * SUB, m * ny : (m + 1) * ny
                ]

    z = column_of(rate, lambda i: i % modes, rows) * (1.0 / extent)
    g = gain(z)
    full = (rows, ny)
    r = jnp.broadcast_to(jnp.exp(-z), full)
    pass_gain = jnp.broadcast_to((g * g) * (g * g), full)
    zeros = (jnp.zeros(full, F32),) * ORDER

    def onward(x, states):
        at = pl.ds(pl.multiple_of(x * rows, SUB), rows)
        value = n_ref[pl.ds(x, rows, stride=nx), :]
        proj_ref[at, :] = value
        states = section(r, states, value)
        y_ref[at, :] = states[-1] * pass_gain
        return states

    def backward(n, states):
        x = nx - 1 - n
        return section(r, states, y_ref[pl.ds(pl.multiple_of(x * rows, SUB), rows), :])

    ends = lax.fori_loop(0, nx, onward, zeros, unroll=8)
    starts = lax.fori_loop(0, nx, backward, zeros, unroll=8)

    ahead = (blocks - 1 - place) * nx
    span = (blocks - 1) * nx
    span = -(-span // LANES) * LANES
    n = iota((rows, span), 1).astype(F32) + 1.0
    inside = iota((rows, span), 1) < ahead
    weight = jnp.where(inside, jnp.exp(-z * (2.0 * n - 1.0)), 0.0) * ((g * g) * (g * g))
    sums = {}
    for a in range(ORDER):
        for b in range(a, ORDER):
            sums[a, b] = jnp.sum(weight * poly(a, n) * poly(b, n), axis=1, keepdims=True)
            sums[b, a] = sums[a, b]
    hat = [[sums[a, ORDER - 1 - b] for b in range(ORDER)] for a in range(ORDER)]
    lane = iota((rows, LANES), 1)
    packed = jnp.zeros((rows, LANES), F32)
    for a in range(ORDER):
        for b in range(ORDER):
            packed = jnp.where(lane == a * ORDER + b, hat[a][b], packed)
    hat_ref[...] = packed

    turned = [sum(hat[a][b] * ends[b] for b in range(ORDER)) for a in range(ORDER)]
    turned = shifted(power(z, nx), turned)
    leaving = [starts[a] + turned[a] for a in range(ORDER)]
    for d in range(1, blocks):
        to_right = ends if d == 1 else shifted(power(z, (d - 1) * nx), ends)
        hops = blocks - d
        to_left = leaving if hops == 1 else shifted(power(z, (hops - 1) * nx), leaving)
        for a in range(ORDER):
            msg_refs[d - 1][pl.ds(a * rows, rows), :] = jnp.where(
                place + d < blocks, to_right[a], to_left[a]
            )


def table_kernel(blocks, extent, extent_x, e_ref, rx_ref, ry_ref, send_ref, high_ref, low_ref, fix_ref, lift_ref, own_ref, rise_ref, fall_ref):
    modes = e_ref.shape[1]
    ny = high_ref.shape[1]
    place = lax.axis_index("gy")
    states = modes * ORDER

    spread = (iota((modes, LANES), 1) // ORDER == iota((modes, LANES), 0)).astype(F32)
    live = (iota((1, LANES), 1) < states).astype(F32)
    lift = exact(e_ref[...], spread)
    lift_ref[...] = jnp.concatenate([lift, lift], 1)
    z = exact(ry_ref[...], spread) * (1.0 / extent)
    zx = exact(rx_ref[...], spread) * (1.0 / extent_x)
    g = gain(z)
    gx = gain(zx)
    pass_gain = (g * g) * (g * g) * live
    scale = jnp.sqrt((2.0 - g) / jnp.where(live > 0, g, 1.0)) * jnp.sqrt(
        (2.0 - gx) / jnp.where(live > 0, gx, 1.0)
    )
    scale = scale * live
    square = (LANES, LANES)
    eye = iota(square, 0) == iota(square, 1)

    def to_column(row):
        return jnp.sum(jnp.where(eye, jnp.broadcast_to(row, square), 0.0), axis=1, keepdims=True)

    def pick(index, choices):
        out = choices[0]
        for k in range(1, len(choices)):
            out = jnp.where(index == k, choices[k], out)
        return out

    z_col = to_column(z)
    scale_col = to_column(scale)
    gain_col = to_column(pass_gain)
    same = iota(square, 0) // ORDER == iota(square, 1) // ORDER
    row_state = iota(square, 0) % ORDER
    lane_state = iota(square, 1) % ORDER

    def moved(steps):
        if steps == 0:
            return jnp.where(eye, 1.0, 0.0)
        decay = jnp.exp(-z * float(steps))
        up = lane_state - row_state
        by = pick(up, [poly(d, float(steps)) for d in range(ORDER)])
        return jnp.where(same & (up >= 0), decay * by, 0.0)

    ahead = (blocks - 1 - place) * ny
    span = (blocks - 1) * ny
    n = iota((LANES, span), 1).astype(F32) + 1.0
    state = iota((LANES, span), 0) % ORDER
    inside = iota((LANES, span), 1) < ahead
    polys = [poly(d, n) for d in range(ORDER)]
    first = jnp.where(inside, jnp.exp(-z_col * n), 0.0) * pick(state, polys[::-1])
    second = jnp.exp(-z_col * (n - 1.0)) * pick(state, polys)
    hat = jnp.where(same, exact(first, second, ((1,), (1,))), 0.0)

    j = iota((ny, LANES), 0).astype(F32)
    lanes = iota((ny, LANES), 1) % ORDER
    from_end = float(ny) - j
    st = jnp.exp(-z * (from_end - 1.0)) * pick(lanes, [poly(a, from_end) for a in range(ORDER)]) * live
    sbt = jnp.exp(-z * j) * pick(lanes, [poly(a, j + 1.0) for a in range(ORDER)]) * live
    c_n = float(ny) - iota((LANES, ny), 1).astype(F32)
    c_state = iota((LANES, ny), 0) % ORDER
    cbt = jnp.exp(-z_col * c_n) * pick(c_state, [poly(ORDER - 1 - a, c_n) for a in range(ORDER)])
    bent = exact(st, hat)
    own_ref[...] = hat * pass_gain

    gap = iota((ny, ny), 1) - iota((ny, ny), 0)
    rise = jnp.maximum(gap, 0).astype(F32)
    fall = jnp.maximum(-gap, 0).astype(F32)
    rise_ref[...] = jnp.where(gap >= 0, poly(ORDER - 1, rise + 1.0), 0.0)
    fall_ref[...] = jnp.where(gap <= 0, poly(ORDER - 1, fall + 1.0), 0.0)
    group = iota((ny, LANES), 1) // ORDER
    edge = split(sbt)
    seen = jnp.zeros((ny, LANES), F32)
    for k in range(modes):
        rate = -z[:, k * ORDER : k * ORDER + 1]
        up = split(jnp.exp(rise * rate) * rise_ref[...])
        down = split(jnp.exp(fall * rate) * fall_ref[...])
        both = dot3(up, [jnp.concatenate([down[i], edge[i]], 1) for i in range(2)])
        high_ref[k], low_ref[k] = split(both[:, :ny])
        seen = jnp.where(group == k, both[:, ny:], seen)

    leaving = (seen + exact(bent, moved(ny))) * (pass_gain * pass_gain)
    wide = jnp.zeros(send_ref.shape, F32)
    for d in range(1, blocks):
        ends = float(d * ny) - j
        to_right = jnp.exp(-z * (ends - 1.0)) * pick(lanes, [poly(a, ends) for a in range(ORDER)]) * pass_gain
        to_left = exact(leaving, moved((blocks - d - 1) * ny))
        chosen = jnp.where(place + d < blocks, to_right, to_left)
        pad = jnp.zeros((ny, send_ref.shape[1] - LANES), F32)
        chosen = jnp.concatenate([chosen, pad], 1) if pad.shape[1] else chosen
        wide = wide + (pltpu.roll(chosen, (d - 1) * states, 1) if d > 1 else chosen)
    send_ref[...] = wide

    flip = same & (row_state + lane_state == ORDER - 1)
    turned = exact(jnp.where(flip, jnp.exp(-z_col), 0.0), seen, ((1,), (1,)))
    bent_on = exact(exact(moved(ny), hat), cbt)
    fix_ref[0:LANES, :] = (turned + bent_on) * (gain_col * scale_col)
    fix_ref[LANES : 2 * LANES, :] = cbt * scale_col


def x_kernel(blocks, blocks_y, extent, proj_ref, hat_ref, rx_ref, send_ref, *refs):
    got = refs[: blocks - 1]
    f_ref, msg_refs, y_ref, z_ref = refs[blocks - 1], refs[blocks:-2], refs[-2], refs[-1]
    rows = hat_ref.shape[0]
    modes = rx_ref.shape[1]
    members = rows // modes
    ny = proj_ref.shape[1]
    nx = proj_ref.shape[0] // rows
    place = lax.axis_index("gx")
    full = (rows, ny)
    z = column_of(rx_ref[...], lambda i: i % modes, rows) * (1.0 / extent)
    g = gain(z)
    r = jnp.broadcast_to(jnp.exp(-z), full)
    pass_gain = jnp.broadcast_to((g * g) * (g * g), full)

    left, right = [], []
    for a in range(ORDER):
        e = jnp.zeros(full, F32)
        b = jnp.zeros(full, F32)
        for d in range(1, blocks):
            value = got[d - 1][pl.ds(a * rows, rows), :]
            e = e + jnp.where(place >= d, value, 0.0)
            b = b + jnp.where(place >= d, 0.0, value)
        left.append(e)
        right.append(b)

    def onward(x, states):
        at = pl.ds(pl.multiple_of(x * rows, SUB), rows)
        states = section(r, states, proj_ref[at, :])
        y_ref[at, :] = states[-1] * pass_gain
        return states

    def backward(n, states):
        x = nx - 1 - n
        at = pl.ds(pl.multiple_of(x * rows, SUB), rows)
        states = section(r, states, y_ref[at, :])
        z_ref[at, :] = states[-1]
        return states

    ends = lax.fori_loop(0, nx, onward, tuple(left), unroll=8)
    hat = hat_ref[...]
    for a in range(ORDER):
        for b in range(ORDER):
            at = a * ORDER + b
            right[a] = right[a] + hat[:, at : at + 1] * ends[b]
    lax.fori_loop(0, nx, backward, tuple(right), unroll=8)

    for k in range(modes):
        for m in range(members):
            f_ref[pl.ds((k * members + m) * nx, nx), :] = z_ref[pl.ds(m * modes + k, nx, stride=rows), :]
    lines = members * nx
    wide = dot3(split(f_ref[...]), split(send_ref[...]))
    states = modes * ORDER
    group = (iota((lines, wide.shape[1]), 1) % states) // ORDER
    total = jnp.zeros(group.shape, F32)
    for k in range(modes):
        total = jnp.where(group == k, wide[k * lines : (k + 1) * lines], total)
    for d in range(blocks_y - 1):
        moved = pltpu.roll(total, total.shape[1] - d * states, 1) if d else total
        msg_refs[d][...] = moved[:, :LANES]


def local_kernel(extent, extent_x, z_ref, high_ref, low_ref, e_ref, rx_ref, ry_ref, out_ref, f_ref):
    levels, modes = e_ref.shape
    members = out_ref.shape[0] // levels
    nx = out_ref.shape[1]
    ny = z_ref.shape[1]
    lines = members * nx
    for k in range(modes):
        high, low = split(z_ref[pl.ds(k * lines, lines), :])
        wide = dot(high, jnp.concatenate([high_ref[k], low_ref[k]], 1))
        f_ref[pl.ds(k * lines, lines), :] = wide[:, :ny] + (wide[:, ny:] + dot(low, high_ref[k]))
    g = gain(ry_ref[...] * (1.0 / extent))
    gx = gain(rx_ref[...] * (1.0 / extent_x))
    pass_gain = (g * g) * (g * g)
    scale = jnp.sqrt((2.0 - g) / g) * jnp.sqrt((2.0 - gx) / gx) * pass_gain * pass_gain
    mix = split(expanded(e_ref[...] * scale, levels, modes))
    for t in range(nx // SUB):
        wide = jnp.concatenate(
            [
                jnp.concatenate(
                    [f_ref[pl.ds(k * lines + m * nx + t * SUB, SUB), :] for k in range(modes)], 0
                )
                for m in range(members)
            ],
            1,
        )
        done = dot3(mix, split(wide))
        for m in range(members):
            for l in range(levels):
                out_ref[m * levels + l, pl.ds(t * SUB, SUB), :] = done[
                    l * SUB : (l + 1) * SUB, m * ny : (m + 1) * ny
                ]


def final_kernel(blocks, total_members, p_ref, base_ref, fix_ref, lift_ref, own_ref, sent_ref, *refs):
    got, out_ref = refs[:-1], refs[-1]
    members, levels, nx, ny = p_ref.shape
    place = lax.axis_index("gy")
    left = jnp.zeros(got[0].shape, F32)
    right = exact(sent_ref[...], own_ref[...])
    for d in range(1, blocks):
        value = got[d - 1][...]
        left = left + jnp.where(place >= d, value, 0.0)
        right = right + jnp.where(place >= d, 0.0, value)
    enter = jnp.concatenate([left, right], 1)
    fix = split(fix_ref[...])
    share = 1.0 / (total_members - 1)
    for l in range(levels):
        add = dot3(split(enter * lift_ref[pl.ds(l, 1), :]), fix)
        out = jnp.zeros((nx, ny), F32)
        for m in range(members):
            out = out + p_ref[m, l].astype(F32) * (
                base_ref[m * levels + l] + add[m * nx : (m + 1) * nx]
            )
        out_ref[l] = out * share


def call(kernel, out, ins, scratch=(), far=False, flops=0, name=None):
    spec = lambda i: pl.BlockSpec(memory_space=pltpu.HBM if far else VMEM)
    nbytes = sum(a.size * a.dtype.itemsize for a in ins) + sum(
        a.size * a.dtype.itemsize for a in jax.tree.leaves(out)
    )
    return pl.pallas_call(
        kernel,
        out_shape=out,
        in_specs=[spec(i) for i in range(len(ins))],
        out_specs=jax.tree.map(lambda _: pl.BlockSpec(memory_space=VMEM), out),
        scratch_shapes=list(scratch),
        cost_estimate=pl.CostEstimate(flops=flops, bytes_accessed=nbytes, transcendentals=0),
        compiler_params=pltpu.CompilerParams(vmem_limit_bytes=GRANT),
        name=name,
    )(*ins)


def shape(*dims):
    return jax.ShapeDtypeStruct(dims, F32)


def turn(value, axis, distance):
    n = lax.axis_size(axis)
    return lax.ppermute(value, axis, [(i, (i + distance) % n) for i in range(n)])


def body(perturb, gradient, vertical_eigenmodes, rate_x, rate_y):
    members, levels, nx, ny = perturb.shape
    modes = vertical_eigenmodes.shape[1]
    rows = members * modes
    blocks_x, blocks_y = lax.axis_size("gx"), lax.axis_size("gy")
    extent_x, extent_y = nx * blocks_x, ny * blocks_y

    proj, hat, eigen, row_x, row_y, *messages = call(
        functools.partial(project_kernel, blocks_x, extent_x),
        tuple(
            [shape(rows * nx, ny), shape(rows, LANES), shape(levels, modes), shape(1, modes), shape(1, modes)]
            + [shape(ORDER * rows, ny)] * (blocks_x - 1)
        ),
        tuple(
            pltpu.with_memory_space_constraint(a, pltpu.HBM)
            for a in (perturb, gradient, vertical_eigenmodes, rate_x[None, :], rate_y[None, :])
        ),
        scratch=(
            VMEM(perturb.shape, perturb.dtype),
            VMEM(gradient.shape, F32),
            VMEM((members * levels * nx, ny), F32),
            VMEM((rows * nx, ny), F32),
            VMEM((rows * nx, ny), F32),
            pltpu.SemaphoreType.DMA((4 + members,)),
        ),
        far=True,
        flops=1 << 28,
        name="project",
    )
    got = [turn(messages[d - 1], "gx", d) for d in range(1, blocks_x)]
    packed = -(-(blocks_y - 1) * modes * ORDER // LANES) * LANES
    half = jax.ShapeDtypeStruct((modes, ny, ny), BF16)
    send, high, low, fix, lift, own = call(
        functools.partial(table_kernel, blocks_y, extent_y, extent_x),
        (shape(ny, packed), half, half, shape(2 * LANES, ny), shape(levels, 2 * LANES), shape(LANES, LANES)),
        (eigen, row_x, row_y),
        scratch=(VMEM((ny, ny), F32), VMEM((ny, ny), F32)),
        flops=1 << 30,
        name="tables",
    )
    filtered, *sent = call(
        functools.partial(x_kernel, blocks_x, blocks_y, extent_x),
        tuple([shape(rows * nx, ny)] + [shape(members * nx, LANES)] * (blocks_y - 1)),
        (proj, hat, row_x, send, *got),
        scratch=(VMEM((rows * nx, ny), F32), VMEM((rows * nx, ny), F32)),
        flops=1 << 28,
        name="along_x",
    )
    got = [turn(sent[d - 1], "gy", d) for d in range(1, blocks_y)]
    base = call(
        functools.partial(local_kernel, extent_y, extent_x),
        shape(members * levels, nx, ny),
        (filtered, high, low, eigen, row_x, row_y),
        scratch=(VMEM((rows * nx, ny), F32),),
        flops=1 << 29,
        name="along_y",
    )
    partial = call(
        functools.partial(final_kernel, blocks_y, members * lax.axis_size("member")),
        shape(levels, nx, ny),
        (perturb, base, fix, lift, own, sent[0], *got),
        flops=1 << 28,
        name="restore",
    )
    if lax.axis_size("member") == 2:
        return partial + turn(partial, "member", 1)
    return lax.psum(partial, "member")


def solution(mesh):
    return jax.shard_map(
        body,
        mesh=mesh,
        in_specs=(P("member", None, "gx", "gy"), P(None, "gx", "gy"), P(), P(), P()),
        out_specs=P(None, "gx", "gy"),
        check_vma=False,
    )
```

```python
import functools

import jax
import jax.numpy as jnp
from jax import lax
from jax.experimental import pallas as pl
from jax.experimental.pallas import tpu as pltpu
from jax.sharding import PartitionSpec as P

F32 = jnp.float32
BF16 = jnp.bfloat16
VMEM = pltpu.VMEM
ORDER = 4
LANES = 128
SUB = 8
GRANT = 12 << 20


def poly(d, n):
    if d == 0:
        return jnp.ones_like(n) if hasattr(n, "shape") else 1.0
    if d == 1:
        return n
    if d == 2:
        return n * (n + 1.0) * 0.5
    return n * (n + 1.0) * (n + 2.0) * (1.0 / 6.0)


def gain(z):
    series = jnp.ones_like(z)
    for k in range(12, 1, -1):
        series = 1.0 - z * series * (1.0 / k)
    return jnp.where(z < 1.0, z * series, 1.0 - jnp.exp(-z))


def split(a):
    high = a.astype(BF16)
    return high, (a - high.astype(F32)).astype(BF16)


def dot(a, b):
    return jnp.dot(a, b, preferred_element_type=F32)


def dot3(a, b):
    return dot(jnp.concatenate([a[0], a[0], a[1]], 1), jnp.concatenate([b[0], b[1], b[0]], 0))


def exact(a, b, contract=((1,), (0,))):
    return lax.dot_general(
        a, b, (contract, ((), ())), precision=lax.Precision.HIGHEST, preferred_element_type=F32
    )


def iota(shape, axis):
    return lax.broadcasted_iota(jnp.int32, shape, axis)


def column_of(row, pick, rows):
    n = row.shape[1]
    wide = jnp.broadcast_to(row, (rows, n))
    hit = iota((rows, n), 1) == pick(iota((rows, n), 0))
    return jnp.sum(jnp.where(hit, wide, 0.0), axis=1, keepdims=True)


def expanded(matrix, rows, cols):
    left = (iota((rows * SUB, rows), 0) // SUB == iota((rows * SUB, rows), 1)).astype(F32)
    right = (iota((cols, cols * SUB), 1) // SUB == iota((cols, cols * SUB), 0)).astype(F32)
    full = exact(exact(left, matrix), right)
    shape = (rows * SUB, cols * SUB)
    return jnp.where(iota(shape, 0) % SUB == iota(shape, 1) % SUB, full, 0.0)


def shifted(coefficients, states):
    out = []
    for a in range(ORDER):
        total = coefficients[0] * states[a]
        for c in range(a):
            total = total + coefficients[a - c] * states[c]
        out.append(total)
    return out


def power(z, steps):
    decay = jnp.exp(-z * float(steps))
    return [decay * poly(d, float(steps)) for d in range(ORDER)]


def target(place, d, blocks):
    if blocks & (blocks - 1) == 0:
        return place ^ d
    return (place + d) % blocks


def source(place, d, blocks):
    if blocks & (blocks - 1) == 0:
        return place ^ d
    return (place - d + blocks) % blocks


def section(r, states, value):
    out = []
    for s in states:
        value = r * s + value
        out.append(value)
    return tuple(out)


def project_kernel(blocks, extent, p_hbm, g_hbm, e_hbm, rx_hbm, ry_hbm, proj_ref, z_ref, end_ref, hat_ref, e_ref, rx_ref, ry_ref, *refs):
    msg_refs = refs[: blocks - 1]
    p_ref, g_ref, mix_ref, n_ref, y_ref, sems = refs[blocks - 1 :]
    members, levels, nx, ny = p_ref.shape
    modes = e_ref.shape[1]
    rows = members * modes
    place = lax.axis_index("gx")
    depth = 2 * SUB if nx % (2 * SUB) == 0 else SUB
    pairs = [(e_hbm, e_ref), (rx_hbm, rx_ref), (ry_hbm, ry_ref), (g_hbm, g_ref), (p_hbm, p_ref)]
    copies = [pltpu.make_async_copy(a, b, sems.at[i]) for i, (a, b) in enumerate(pairs)]
    for copy in copies:
        copy.start()
    for copy in copies[:3]:
        copy.wait()
    rate = rx_ref[...]
    pitch = n_ref.shape[0] // rows

    z_rows = column_of(rate, lambda i: i // SUB, modes * SUB) * (1.0 / extent)
    g_rows = gain(z_rows)
    mix = split(expanded(e_ref[...].T, modes, levels) * (g_rows * g_rows) * (g_rows * g_rows))
    mix_ref[...] = jnp.concatenate([mix[0], mix[0], mix[1]], 1)

    z = column_of(rate, lambda i: i % modes, rows) * (1.0 / extent)
    g = gain(z)
    full = (rows, ny)
    r = jnp.broadcast_to(jnp.exp(-z), full)
    pass_gain = jnp.broadcast_to((g * g) * (g * g), full)
    zeros = (jnp.zeros(full, F32),) * ORDER

    ahead = (blocks - 1 - place) * nx
    span = (blocks - 1) * nx
    span = -(-span // LANES) * LANES
    n = iota((rows, span), 1).astype(F32) + 1.0
    inside = iota((rows, span), 1) < ahead
    weight = jnp.where(inside, jnp.exp(-z * (2.0 * n - 1.0)), 0.0) * ((g * g) * (g * g))
    sums = {}
    for a in range(ORDER):
        for b in range(a, ORDER):
            sums[a, b] = jnp.sum(weight * poly(a, n) * poly(b, n), axis=1, keepdims=True)
            sums[b, a] = sums[a, b]
    hat = [[sums[a, ORDER - 1 - b] for b in range(ORDER)] for a in range(ORDER)]
    lane = iota((rows, LANES), 1)
    packed = jnp.zeros((rows, LANES), F32)
    for a in range(ORDER):
        for b in range(ORDER):
            packed = jnp.where(lane == a * ORDER + b, hat[a][b], packed)
    hat_ref[...] = packed

    for copy in copies[3:]:
        copy.wait()
    for t in range(nx // depth):
        at = pl.ds(t * depth, depth)
        parts = [
            [p_ref[m, l, at, :].astype(F32) * g_ref[l, at, :] for l in range(levels)]
            for m in range(members)
        ]
        for h in range(depth // SUB):
            wide = jnp.concatenate(
                [
                    jnp.concatenate([part[h * SUB : (h + 1) * SUB] for part in parts[m]], 0)
                    for m in range(members)
                ],
                1,
            )
            high, low = split(wide)
            done = dot(mix_ref[...], jnp.concatenate([high, low, high], 0))
            for m in range(members):
                for k in range(modes):
                    at = pl.ds((m * modes + k) * pitch + t * depth + h * SUB, SUB)
                    n_ref[at, :] = done[k * SUB : (k + 1) * SUB, m * ny : (m + 1) * ny]

    def onward(x, states):
        at = pl.ds(pl.multiple_of(x * rows, SUB), rows)
        value = n_ref[pl.ds(x, rows, stride=pitch), :]
        proj_ref[at, :] = value
        states = section(r, states, value)
        y_ref[at, :] = states[-1] * pass_gain
        return states

    def backward(n, states):
        at = pl.ds(pl.multiple_of((nx - 1 - n) * rows, SUB), rows)
        states = section(r, states, y_ref[at, :])
        z_ref[at, :] = states[-1]
        return states

    ends = lax.fori_loop(0, nx, onward, zeros, unroll=8)
    starts = lax.fori_loop(0, nx, backward, zeros, unroll=8)

    turned = [sum(hat[a][b] * ends[b] for b in range(ORDER)) for a in range(ORDER)]
    turned = shifted(power(z, nx), turned)
    leaving = [starts[a] + turned[a] for a in range(ORDER)]
    for a in range(ORDER):
        end_ref[pl.ds(a * rows, rows), :] = ends[a]
    to_right, to_left = {1: ends}, {1: leaving}
    for hops in range(2, blocks):
        over = power(z, (hops - 1) * nx)
        to_right[hops] = shifted(over, ends)
        to_left[hops] = shifted(over, leaving)
    for d in range(1, blocks):
        to = target(place, d, blocks)
        reach = sorted({abs(target(i, d, blocks) - i) for i in range(blocks)})
        for a in range(ORDER):
            value = to_right[reach[0]][a]
            for hops in reach:
                value = jnp.where(to - place == hops, to_right[hops][a], value)
                value = jnp.where(place - to == hops, to_left[hops][a], value)
            msg_refs[d - 1][pl.ds(a * rows, rows), :] = value


def table_kernel(blocks, extent, extent_x, e_ref, rx_ref, ry_ref, send_ref, high_ref, low_ref, fix_ref, lift_ref, own_ref):
    modes = e_ref.shape[1]
    ny = high_ref.shape[1]
    place = lax.axis_index("gy")
    states = modes * ORDER

    spread = (iota((modes, LANES), 1) // ORDER == iota((modes, LANES), 0)).astype(F32)
    live = (iota((1, LANES), 1) < states).astype(F32)
    lift = exact(e_ref[...], spread)
    lift_ref[...] = jnp.concatenate([lift, lift], 1)
    z = exact(ry_ref[...], spread) * (1.0 / extent)
    zx = exact(rx_ref[...], spread) * (1.0 / extent_x)
    g = gain(z)
    gx = gain(zx)
    pass_gain = (g * g) * (g * g) * live
    scale = jnp.sqrt((2.0 - g) / jnp.where(live > 0, g, 1.0)) * jnp.sqrt(
        (2.0 - gx) / jnp.where(live > 0, gx, 1.0)
    )
    scale = scale * live
    square = (LANES, LANES)
    eye = iota(square, 0) == iota(square, 1)

    def to_column(row):
        return jnp.sum(jnp.where(eye, jnp.broadcast_to(row, square), 0.0), axis=1, keepdims=True)

    def pick(index, choices):
        out = choices[0]
        for k in range(1, len(choices)):
            out = jnp.where(index == k, choices[k], out)
        return out

    z_col = to_column(z)
    scale_col = to_column(scale)
    gain_col = to_column(pass_gain)
    same = iota(square, 0) // ORDER == iota(square, 1) // ORDER
    row_state = iota(square, 0) % ORDER
    lane_state = iota(square, 1) % ORDER

    def moved(steps):
        if steps == 0:
            return jnp.where(eye, 1.0, 0.0)
        decay = jnp.exp(-z * float(steps))
        up = lane_state - row_state
        by = pick(up, [poly(d, float(steps)) for d in range(ORDER)])
        return jnp.where(same & (up >= 0), decay * by, 0.0)

    ahead = (blocks - 1 - place) * ny
    span = (blocks - 1) * ny
    n = iota((LANES, span), 1).astype(F32) + 1.0
    state = iota((LANES, span), 0) % ORDER
    inside = iota((LANES, span), 1) < ahead
    polys = [poly(d, n) for d in range(ORDER)]
    first = jnp.where(inside, jnp.exp(-z_col * n), 0.0) * pick(state, polys[::-1])
    second = jnp.exp(-z_col * (n - 1.0)) * pick(state, polys)
    hat = jnp.where(same, exact(first, second, ((1,), (1,))), 0.0)

    j = iota((ny, LANES), 0).astype(F32)
    lanes = iota((ny, LANES), 1) % ORDER
    from_end = float(ny) - j
    st = jnp.exp(-z * (from_end - 1.0)) * pick(lanes, [poly(a, from_end) for a in range(ORDER)]) * live
    sbt = jnp.exp(-z * j) * pick(lanes, [poly(a, j + 1.0) for a in range(ORDER)]) * live
    c_n = float(ny) - iota((LANES, ny), 1).astype(F32)
    c_state = iota((LANES, ny), 0) % ORDER
    cbt = jnp.exp(-z_col * c_n) * pick(c_state, [poly(ORDER - 1 - a, c_n) for a in range(ORDER)])
    bent = exact(st, hat)
    own_ref[...] = hat * pass_gain

    gap = iota((ny, ny), 1) - iota((ny, ny), 0)
    z_mode = ry_ref[...] * (1.0 / extent)
    z_mode = jnp.sum(
        jnp.where(
            iota((modes, modes), 0) == iota((modes, modes), 1), jnp.broadcast_to(z_mode, (modes, modes)), 0.0
        ),
        axis=1,
        keepdims=True,
    )
    lag = iota((modes, ny), 1)
    back = jnp.where(lag == 0, 0, ny - lag).astype(F32)
    lag = lag.astype(F32)
    ahead_row = split(jnp.exp(-z_mode * lag) * poly(ORDER - 1, lag + 1.0))
    back_row = split(jnp.exp(-z_mode * back) * poly(ORDER - 1, back + 1.0))
    ahead_row = [part.astype(F32) for part in ahead_row]
    back_row = [part.astype(F32) for part in back_row]

    def band(row, inside):
        wide = jnp.broadcast_to(row, (ny, ny))
        wide = pltpu.roll(wide, 0, 1, stride=1, stride_axis=0)
        return jnp.where(inside, wide, 0.0).astype(BF16)

    group = iota((ny, LANES), 1) // ORDER
    edge = split(sbt)
    seen = jnp.zeros((ny, LANES), F32)
    for k in range(modes):
        up = [band(part[k : k + 1], gap >= 0) for part in ahead_row]
        down = [band(part[k : k + 1], gap <= 0) for part in back_row]
        both = dot3(up, [jnp.concatenate([down[i], edge[i]], 1) for i in range(2)])
        high_ref[k], low_ref[k] = split(both[:, :ny])
        seen = jnp.where(group == k, both[:, ny:], seen)

    leaving = (seen + exact(bent, moved(ny))) * (pass_gain * pass_gain)
    wide = jnp.zeros(send_ref.shape, F32)
    for d in range(1, blocks):
        ends = float(d * ny) - j
        to_right = jnp.exp(-z * (ends - 1.0)) * pick(lanes, [poly(a, ends) for a in range(ORDER)]) * pass_gain
        to_left = exact(leaving, moved((blocks - d - 1) * ny))
        chosen = jnp.where(place + d < blocks, to_right, to_left)
        pad = jnp.zeros((ny, send_ref.shape[1] - LANES), F32)
        chosen = jnp.concatenate([chosen, pad], 1) if pad.shape[1] else chosen
        wide = wide + (pltpu.roll(chosen, (d - 1) * states, 1) if d > 1 else chosen)
    send_ref[...] = wide

    flip = same & (row_state + lane_state == ORDER - 1)
    turned = exact(jnp.where(flip, jnp.exp(-z_col), 0.0), seen, ((1,), (1,)))
    bent_on = exact(exact(moved(ny), hat), cbt)
    fix = jnp.concatenate([(turned + bent_on) * (gain_col * scale_col), cbt * scale_col], 0)
    high, low = split(fix)
    fix_ref[...] = jnp.concatenate([high, low, high], 0)


def lane_group(shape, modes):
    return (iota(shape, len(shape) - 1) % (modes * ORDER)) // ORDER


def by_mode(f_ref, z_ref, members, modes, nx):
    for k in range(modes):
        for m in range(members):
            f_ref[pl.ds((k * members + m) * nx, nx), :] = z_ref[
                pl.ds(m * modes + k, nx, stride=members * modes), :
            ]


def early_kernel(extent, z_ref, send_ref, rx_ref, pre_ref, react_ref, f_ref, y_ref, w_ref):
    modes = rx_ref.shape[1]
    nx = react_ref.shape[0] // (2 * ORDER)
    rows = z_ref.shape[0] // nx
    members = rows // modes
    lines = members * nx
    lanes = send_ref.shape[1]
    by_mode(f_ref, z_ref, members, modes, nx)
    wide = dot3(split(f_ref[...]), split(send_ref[...]))
    group = lane_group((lines, lanes), modes)
    total = jnp.zeros(group.shape, F32)
    for k in range(modes):
        total = jnp.where(group == k, wide[k * lines : (k + 1) * lines], total)
    pre_ref[...] = total

    full = (2 * ORDER, lanes)
    spread = (lane_group((modes, lanes), modes) == iota((modes, lanes), 0)).astype(F32)
    z = exact(rx_ref[...], spread) * (1.0 / extent)
    g = gain(z)
    r = jnp.broadcast_to(jnp.exp(-z), full)
    pass_gain = jnp.broadcast_to((g * g) * (g * g), full)
    unit = iota(full, 0)
    zeros = jnp.zeros(full, F32)

    def onward(x, states):
        states = section(r, states, zeros)
        y_ref[pl.ds(pl.multiple_of(x * SUB, SUB), SUB), :] = states[-1] * pass_gain
        return states

    def backward(n, states):
        at = pl.ds(pl.multiple_of((nx - 1 - n) * SUB, SUB), SUB)
        states = section(r, states, y_ref[at, :])
        for t in range(lanes // LANES):
            w_ref[t, at, :] = states[-1][:, t * LANES : (t + 1) * LANES]
        return states

    first = tuple((unit == a).astype(F32) for a in range(ORDER))
    lax.fori_loop(0, nx, onward, first, unroll=8)
    first = tuple((unit == ORDER + a).astype(F32) for a in range(ORDER))
    lax.fori_loop(0, nx, backward, first, unroll=8)
    for a in range(2 * ORDER):
        for t in range(lanes // LANES):
            react_ref[pl.ds(a * nx, nx), t * LANES : (t + 1) * LANES] = w_ref[t, pl.ds(a, nx, stride=SUB), :]


def x_kernel(blocks, blocks_y, extent, end_ref, hat_ref, rx_ref, send_ref, pre_ref, react_ref, *refs):
    got = refs[: blocks - 1]
    enter_ref, msg_refs = refs[blocks - 1], refs[blocks:]
    rows = hat_ref.shape[0]
    modes = rx_ref.shape[1]
    members = rows // modes
    ny = end_ref.shape[1]
    nx = pre_ref.shape[0] // members
    place = lax.axis_index("gx")
    full = (rows, ny)
    z = column_of(rx_ref[...], lambda i: i % modes, rows) * (1.0 / extent)

    left, right = [], []
    for a in range(ORDER):
        e = jnp.zeros(full, F32)
        b = jnp.zeros(full, F32)
        for d in range(1, blocks):
            value = got[d - 1][pl.ds(a * rows, rows), :]
            behind = source(place, d, blocks) < place
            e = e + jnp.where(behind, value, 0.0)
            b = b + jnp.where(behind, 0.0, value)
        left.append(e)
        right.append(b)
    ends = shifted(power(z, nx), left)
    ends = [ends[a] + end_ref[pl.ds(a * rows, rows), :] for a in range(ORDER)]
    hat = hat_ref[...]
    for a in range(ORDER):
        for b in range(ORDER):
            at = a * ORDER + b
            right[a] = right[a] + hat[:, at : at + 1] * ends[b]
    enter = jnp.concatenate(left + right, 0)
    enter_ref[...] = enter

    wide = dot3(split(enter), split(send_ref[...]))
    lanes = wide.shape[1]
    row = iota((rows, lanes), 0)
    mine = row % modes == lane_group((rows, lanes), modes)
    states = modes * ORDER
    for m in range(members):
        here = mine & (row // modes == m)
        total = pre_ref[pl.ds(m * nx, nx), :]
        for a in range(2 * ORDER):
            value = jnp.where(here, wide[a * rows : (a + 1) * rows], 0.0)
            value = jnp.sum(value, axis=0, keepdims=True)
            total = total + react_ref[pl.ds(a * nx, nx), :] * value
        for d in range(blocks_y - 1):
            moved = pltpu.roll(total, lanes - d * states, 1) if d else total
            msg_refs[d][pl.ds(m * nx, nx), :] = moved[:, :LANES]


def local_kernel(extent, extent_x, proj_ref, enter_ref, high_ref, low_ref, e_ref, rx_ref, ry_ref, sent_ref, own_ref, out_ref, right_ref, y_ref, z_ref, f_ref):
    levels, modes = e_ref.shape
    members = out_ref.shape[0] // levels
    rows = members * modes
    nx = out_ref.shape[1]
    ny = proj_ref.shape[1]
    lines = members * nx
    full = (rows, ny)
    z = column_of(rx_ref[...], lambda i: i % modes, rows) * (1.0 / extent_x)
    g = gain(z)
    r = jnp.broadcast_to(jnp.exp(-z), full)
    pass_gain = jnp.broadcast_to((g * g) * (g * g), full)

    def onward(x, states):
        at = pl.ds(pl.multiple_of(x * rows, SUB), rows)
        states = section(r, states, proj_ref[at, :])
        y_ref[at, :] = states[-1] * pass_gain
        return states

    def backward(n, states):
        at = pl.ds(pl.multiple_of((nx - 1 - n) * rows, SUB), rows)
        states = section(r, states, y_ref[at, :])
        z_ref[at, :] = states[-1]
        return states

    left = tuple(enter_ref[pl.ds(a * rows, rows), :] for a in range(ORDER))
    lax.fori_loop(0, nx, onward, left, unroll=8)
    right = tuple(enter_ref[pl.ds((ORDER + a) * rows, rows), :] for a in range(ORDER))
    lax.fori_loop(0, nx, backward, right, unroll=8)

    right_ref[...] = exact(sent_ref[...], own_ref[...])
    by_mode(f_ref, z_ref, members, modes, nx)
    for k in range(modes):
        at = pl.ds(k * lines, lines)
        f_ref[at, :] = dot3(split(f_ref[at, :]), (high_ref[k], low_ref[k]))
    g = gain(ry_ref[...] * (1.0 / extent))
    gx = gain(rx_ref[...] * (1.0 / extent_x))
    pass_gain = (g * g) * (g * g)
    scale = jnp.sqrt((2.0 - g) / g) * jnp.sqrt((2.0 - gx) / gx) * pass_gain * pass_gain
    mix = split(expanded(e_ref[...] * scale, levels, modes))
    for t in range(nx // SUB):
        wide = jnp.concatenate(
            [
                jnp.concatenate(
                    [f_ref[pl.ds(k * lines + m * nx + t * SUB, SUB), :] for k in range(modes)], 0
                )
                for m in range(members)
            ],
            1,
        )
        done = dot3(mix, split(wide))
        for m in range(members):
            for l in range(levels):
                out_ref[m * levels + l, pl.ds(t * SUB, SUB), :] = done[
                    l * SUB : (l + 1) * SUB, m * ny : (m + 1) * ny
                ]


def final_kernel(blocks, total_members, first, p_ref, base_ref, right_ref, fix_ref, lift_ref, *refs):
    got, out_ref = refs[:-1], refs[-1]
    members, levels, nx, ny = p_ref.shape
    place = lax.axis_index("gy")
    left = jnp.zeros(got[0].shape, F32)
    right = right_ref[...]
    for d in range(1, blocks):
        value = got[d - 1][...]
        left = left + jnp.where(place >= d, value, 0.0)
        right = right + jnp.where(place >= d, 0.0, value)
    enter = jnp.concatenate([left, right], 1)
    fix = fix_ref[...]
    share = 1.0 / (total_members - 1)
    for l in range(first, first + out_ref.shape[0]):
        high, low = split(enter * lift_ref[pl.ds(l, 1), :])
        add = dot(jnp.concatenate([high, high, low], 1), fix)
        out = jnp.zeros((nx, ny), F32)
        for m in range(members):
            out = out + p_ref[m, l].astype(F32) * (
                base_ref[m * levels + l] + add[m * nx : (m + 1) * nx]
            )
        out_ref[l - first] = out * share


def call(kernel, out, ins, scratch=(), far=False, flops=0, name=None):
    spec = lambda i: pl.BlockSpec(memory_space=pltpu.HBM if far else VMEM)
    nbytes = sum(a.size * a.dtype.itemsize for a in ins) + sum(
        a.size * a.dtype.itemsize for a in jax.tree.leaves(out)
    )
    return pl.pallas_call(
        kernel,
        out_shape=out,
        in_specs=[spec(i) for i in range(len(ins))],
        out_specs=jax.tree.map(lambda _: pl.BlockSpec(memory_space=VMEM), out),
        scratch_shapes=list(scratch),
        cost_estimate=pl.CostEstimate(flops=flops, bytes_accessed=nbytes, transcendentals=0),
        compiler_params=pltpu.CompilerParams(vmem_limit_bytes=GRANT),
        name=name,
    )(*ins)


def shape(*dims):
    return jax.ShapeDtypeStruct(dims, F32)


def exchange(values, axis, order, to):
    n = lax.axis_size(axis)
    got = {
        d: lax.ppermute(values[d - 1], axis, [(i, to(i, d, n)) for i in range(n)]) for d in order
    }
    return [got[d] for d in range(1, n)]


def body(perturb, gradient, vertical_eigenmodes, rate_x, rate_y):
    members, levels, nx, ny = perturb.shape
    modes = vertical_eigenmodes.shape[1]
    rows = members * modes
    blocks_x, blocks_y = lax.axis_size("gx"), lax.axis_size("gy")
    extent_x, extent_y = nx * blocks_x, ny * blocks_y

    field = shape(rows * nx, ny)
    pitch = (nx // SUB | 1) * SUB
    proj, alone, ends, hat, eigen, row_x, row_y, *messages = call(
        functools.partial(project_kernel, blocks_x, extent_x),
        tuple(
            [field, field, shape(ORDER * rows, ny), shape(rows, LANES)]
            + [shape(levels, modes), shape(1, modes), shape(1, modes)]
            + [shape(ORDER * rows, ny)] * (blocks_x - 1)
        ),
        tuple(
            pltpu.with_memory_space_constraint(a, pltpu.HBM)
            for a in (perturb, gradient, vertical_eigenmodes, rate_x[None, :], rate_y[None, :])
        ),
        scratch=(
            VMEM(perturb.shape, perturb.dtype),
            VMEM(gradient.shape, F32),
            VMEM((modes * SUB, 3 * levels * SUB), BF16),
            VMEM((rows * pitch, ny), F32),
            VMEM((rows * nx, ny), F32),
            pltpu.SemaphoreType.DMA((5,)),
        ),
        far=True,
        flops=1 << 28,
        name="project",
    )
    got = exchange(messages, "gx", [1] + list(range(blocks_x - 1, 1, -1)), target)
    packed = -(-(blocks_y - 1) * modes * ORDER // LANES) * LANES
    half = jax.ShapeDtypeStruct((modes, ny, ny), BF16)
    send, high, low, fix, lift, own = call(
        functools.partial(table_kernel, blocks_y, extent_y, extent_x),
        (
            shape(ny, packed),
            half,
            half,
            jax.ShapeDtypeStruct((6 * LANES, ny), BF16),
            shape(levels, 2 * LANES),
            shape(LANES, LANES),
        ),
        (eigen, row_x, row_y),
        flops=1 << 30,
        name="tables",
    )
    before, react = call(
        functools.partial(early_kernel, extent_x),
        (shape(members * nx, packed), shape(2 * ORDER * nx, packed)),
        (alone, send, row_x),
        scratch=(
            VMEM((rows * nx, ny), F32),
            VMEM((SUB * nx, packed), F32),
            VMEM((packed // LANES, SUB * nx, LANES), F32),
        ),
        flops=1 << 29,
        name="early",
    )
    enter, *sent = call(
        functools.partial(x_kernel, blocks_x, blocks_y, extent_x),
        tuple([shape(2 * ORDER * rows, ny)] + [shape(members * nx, LANES)] * (blocks_y - 1)),
        (ends, hat, row_x, send, before, react, *got),
        flops=1 << 27,
        name="along_x",
    )
    got = exchange(sent, "gy", list(range(blocks_y - 1, 0, -1)), lambda i, d, n: (i + d) % n)
    base, right = call(
        functools.partial(local_kernel, extent_y, extent_x),
        (shape(members * levels, nx, ny), shape(members * nx, LANES)),
        (proj, enter, high, low, eigen, row_x, row_y, sent[0], own),
        scratch=(VMEM((rows * nx, ny), F32),) * 3,
        flops=1 << 29,
        name="along_y",
    )
    pieces = 4 if levels % 4 == 0 else 1
    size = levels // pieces
    parts = [
        call(
            functools.partial(final_kernel, blocks_y, members * lax.axis_size("member"), i * size),
            shape(size, nx, ny),
            (perturb, base, right, fix, lift, *got),
            flops=1 << 27,
            name="restore",
        )
        for i in range(pieces)
    ]
    if lax.axis_size("member") > 2:
        return lax.psum(jnp.concatenate(parts, 0), "member")
    others = [lax.ppermute(part, "member", [(0, 1), (1, 0)]) for part in parts]
    return jnp.concatenate([a + b for a, b in zip(parts, others)], 0)


def solution(mesh):
    return jax.shard_map(
        body,
        mesh=mesh,
        in_specs=(P("member", None, "gx", "gy"), P(None, "gx", "gy"), P(), P(), P()),
        out_specs=P(None, "gx", "gy"),
        check_vma=False,
    )
```

```python
import functools

import jax
import jax.numpy as jnp
from jax import lax
from jax.experimental import pallas as pl
from jax.experimental.pallas import tpu as pltpu
from jax.sharding import PartitionSpec as P

F32 = jnp.float32
BF16 = jnp.bfloat16
VMEM = pltpu.VMEM
ORDER = 4
LANES = 128
SUB = 8
GRANT = 12 << 20


def poly(d, n):
    if d == 0:
        return jnp.ones_like(n) if hasattr(n, "shape") else 1.0
    if d == 1:
        return n
    if d == 2:
        return n * (n + 1.0) * 0.5
    return n * (n + 1.0) * (n + 2.0) * (1.0 / 6.0)


def gain(z):
    series = jnp.ones_like(z)
    for k in range(12, 1, -1):
        series = 1.0 - z * series * (1.0 / k)
    return jnp.where(z < 1.0, z * series, 1.0 - jnp.exp(-z))


def split(a):
    high = a.astype(BF16)
    return high, (a - high.astype(F32)).astype(BF16)


def dot(a, b):
    return jnp.dot(a, b, preferred_element_type=F32)


def dot3(a, b):
    return dot(jnp.concatenate([a[0], a[0], a[1]], 1), jnp.concatenate([b[0], b[1], b[0]], 0))


def exact(a, b, contract=((1,), (0,))):
    return lax.dot_general(
        a, b, (contract, ((), ())), precision=lax.Precision.HIGHEST, preferred_element_type=F32
    )


def iota(shape, axis):
    return lax.broadcasted_iota(jnp.int32, shape, axis)


def column_of(row, pick, rows):
    n = row.shape[1]
    wide = jnp.broadcast_to(row, (rows, n))
    hit = iota((rows, n), 1) == pick(iota((rows, n), 0))
    return jnp.sum(jnp.where(hit, wide, 0.0), axis=1, keepdims=True)


def expanded(matrix, rows, cols):
    left = (iota((rows * SUB, rows), 0) // SUB == iota((rows * SUB, rows), 1)).astype(F32)
    right = (iota((cols, cols * SUB), 1) // SUB == iota((cols, cols * SUB), 0)).astype(F32)
    full = exact(exact(left, matrix), right)
    shape = (rows * SUB, cols * SUB)
    return jnp.where(iota(shape, 0) % SUB == iota(shape, 1) % SUB, full, 0.0)


def shifted(coefficients, states):
    out = []
    for a in range(ORDER):
        total = coefficients[0] * states[a]
        for c in range(a):
            total = total + coefficients[a - c] * states[c]
        out.append(total)
    return out


def power(z, steps):
    decay = jnp.exp(-z * float(steps))
    return [decay * poly(d, float(steps)) for d in range(ORDER)]


def target(place, d, blocks):
    if blocks & (blocks - 1) == 0:
        return place ^ d
    return (place + d) % blocks


def source(place, d, blocks):
    if blocks & (blocks - 1) == 0:
        return place ^ d
    return (place - d + blocks) % blocks


def section(r, states, value):
    out = []
    for s in states:
        value = r * s + value
        out.append(value)
    return tuple(out)


def project_kernel(blocks, extent, p_hbm, g_hbm, e_hbm, rx_hbm, ry_hbm, proj_ref, z_ref, end_ref, hat_ref, e_ref, rx_ref, ry_ref, *refs):
    msg_refs = refs[: blocks - 1]
    p_ref, g_ref, mix_ref, n_ref, y_ref, sems = refs[blocks - 1 :]
    members, levels, nx, ny = p_ref.shape
    modes = e_ref.shape[1]
    rows = members * modes
    place = lax.axis_index("gx")
    depth = 2 * SUB if nx % (2 * SUB) == 0 else SUB
    pairs = [(e_hbm, e_ref), (rx_hbm, rx_ref), (ry_hbm, ry_ref), (g_hbm, g_ref), (p_hbm, p_ref)]
    copies = [pltpu.make_async_copy(a, b, sems.at[i]) for i, (a, b) in enumerate(pairs)]
    for copy in copies:
        copy.start()
    for copy in copies[:3]:
        copy.wait()
    rate = rx_ref[...]
    pitch = n_ref.shape[0] // rows

    z_rows = column_of(rate, lambda i: i // SUB, modes * SUB) * (1.0 / extent)
    g_rows = gain(z_rows)
    mix = split(expanded(e_ref[...].T, modes, levels) * (g_rows * g_rows) * (g_rows * g_rows))
    mix_ref[...] = jnp.concatenate([mix[0], mix[0], mix[1]], 1)

    z = column_of(rate, lambda i: i % modes, rows) * (1.0 / extent)
    g = gain(z)
    full = (rows, ny)
    r = jnp.broadcast_to(jnp.exp(-z), full)
    pass_gain = jnp.broadcast_to((g * g) * (g * g), full)
    zeros = (jnp.zeros(full, F32),) * ORDER

    ahead = (blocks - 1 - place) * nx
    span = (blocks - 1) * nx
    span = -(-span // LANES) * LANES
    n = iota((rows, span), 1).astype(F32) + 1.0
    inside = iota((rows, span), 1) < ahead
    weight = jnp.where(inside, jnp.exp(-z * (2.0 * n - 1.0)), 0.0) * ((g * g) * (g * g))
    sums = {}
    for a in range(ORDER):
        for b in range(a, ORDER):
            sums[a, b] = jnp.sum(weight * poly(a, n) * poly(b, n), axis=1, keepdims=True)
            sums[b, a] = sums[a, b]
    hat = [[sums[a, ORDER - 1 - b] for b in range(ORDER)] for a in range(ORDER)]
    lane = iota((rows, LANES), 1)
    packed = jnp.zeros((rows, LANES), F32)
    for a in range(ORDER):
        for b in range(ORDER):
            packed = jnp.where(lane == a * ORDER + b, hat[a][b], packed)
    hat_ref[...] = packed

    for copy in copies[3:]:
        copy.wait()
    for t in range(nx // depth):
        at = pl.ds(t * depth, depth)
        parts = [
            [p_ref[m, l, at, :].astype(F32) * g_ref[l, at, :] for l in range(levels)]
            for m in range(members)
        ]
        for h in range(depth // SUB):
            wide = jnp.concatenate(
                [
                    jnp.concatenate([part[h * SUB : (h + 1) * SUB] for part in parts[m]], 0)
                    for m in range(members)
                ],
                1,
            )
            high, low = split(wide)
            done = dot(mix_ref[...], jnp.concatenate([high, low, high], 0))
            for m in range(members):
                for k in range(modes):
                    at = pl.ds((m * modes + k) * pitch + t * depth + h * SUB, SUB)
                    n_ref[at, :] = done[k * SUB : (k + 1) * SUB, m * ny : (m + 1) * ny]

    def onward(x, states):
        at = pl.ds(pl.multiple_of(x * rows, SUB), rows)
        value = n_ref[pl.ds(x, rows, stride=pitch), :]
        proj_ref[at, :] = value
        states = section(r, states, value)
        y_ref[at, :] = states[-1] * pass_gain
        return states

    def backward(n, states):
        at = pl.ds(pl.multiple_of((nx - 1 - n) * rows, SUB), rows)
        states = section(r, states, y_ref[at, :])
        z_ref[at, :] = states[-1]
        return states

    ends = lax.fori_loop(0, nx, onward, zeros, unroll=8)
    starts = lax.fori_loop(0, nx, backward, zeros, unroll=8)

    turned = [sum(hat[a][b] * ends[b] for b in range(ORDER)) for a in range(ORDER)]
    turned = shifted(power(z, nx), turned)
    leaving = [starts[a] + turned[a] for a in range(ORDER)]
    for a in range(ORDER):
        end_ref[pl.ds(a * rows, rows), :] = ends[a]
    to_right, to_left = {1: ends}, {1: leaving}
    for hops in range(2, blocks):
        over = power(z, (hops - 1) * nx)
        to_right[hops] = shifted(over, ends)
        to_left[hops] = shifted(over, leaving)
    for d in range(1, blocks):
        to = target(place, d, blocks)
        reach = sorted({abs(target(i, d, blocks) - i) for i in range(blocks)})
        for a in range(ORDER):
            value = to_right[reach[0]][a]
            for hops in reach:
                value = jnp.where(to - place == hops, to_right[hops][a], value)
                value = jnp.where(place - to == hops, to_left[hops][a], value)
            msg_refs[d - 1][pl.ds(a * rows, rows), :] = value


def table_kernel(blocks, extent, extent_x, e_ref, rx_ref, ry_ref, send_ref, high_ref, low_ref, fix_ref, lift_ref, own_ref):
    modes = e_ref.shape[1]
    ny = high_ref.shape[1]
    place = lax.axis_index("gy")
    states = modes * ORDER

    spread = (iota((modes, LANES), 1) // ORDER == iota((modes, LANES), 0)).astype(F32)
    live = (iota((1, LANES), 1) < states).astype(F32)
    lift = exact(e_ref[...], spread)
    lift_ref[...] = jnp.concatenate([lift, lift], 1)
    z = exact(ry_ref[...], spread) * (1.0 / extent)
    zx = exact(rx_ref[...], spread) * (1.0 / extent_x)
    g = gain(z)
    gx = gain(zx)
    pass_gain = (g * g) * (g * g) * live
    scale = jnp.sqrt((2.0 - g) / jnp.where(live > 0, g, 1.0)) * jnp.sqrt(
        (2.0 - gx) / jnp.where(live > 0, gx, 1.0)
    )
    scale = scale * live
    square = (LANES, LANES)
    eye = iota(square, 0) == iota(square, 1)

    def to_column(row):
        return jnp.sum(jnp.where(eye, jnp.broadcast_to(row, square), 0.0), axis=1, keepdims=True)

    def pick(index, choices):
        out = choices[0]
        for k in range(1, len(choices)):
            out = jnp.where(index == k, choices[k], out)
        return out

    z_col = to_column(z)
    scale_col = to_column(scale)
    gain_col = to_column(pass_gain)
    same = iota(square, 0) // ORDER == iota(square, 1) // ORDER
    row_state = iota(square, 0) % ORDER
    lane_state = iota(square, 1) % ORDER

    def moved(steps):
        if steps == 0:
            return jnp.where(eye, 1.0, 0.0)
        decay = jnp.exp(-z * float(steps))
        up = lane_state - row_state
        by = pick(up, [poly(d, float(steps)) for d in range(ORDER)])
        return jnp.where(same & (up >= 0), decay * by, 0.0)

    ahead = (blocks - 1 - place) * ny
    span = (blocks - 1) * ny
    n = iota((LANES, span), 1).astype(F32) + 1.0
    state = iota((LANES, span), 0) % ORDER
    inside = iota((LANES, span), 1) < ahead
    polys = [poly(d, n) for d in range(ORDER)]
    first = jnp.where(inside, jnp.exp(-z_col * n), 0.0) * pick(state, polys[::-1])
    second = jnp.exp(-z_col * (n - 1.0)) * pick(state, polys)
    hat = jnp.where(same, exact(first, second, ((1,), (1,))), 0.0)

    j = iota((ny, LANES), 0).astype(F32)
    lanes = iota((ny, LANES), 1) % ORDER
    from_end = float(ny) - j
    st = jnp.exp(-z * (from_end - 1.0)) * pick(lanes, [poly(a, from_end) for a in range(ORDER)]) * live
    sbt = jnp.exp(-z * j) * pick(lanes, [poly(a, j + 1.0) for a in range(ORDER)]) * live
    c_n = float(ny) - iota((LANES, ny), 1).astype(F32)
    c_state = iota((LANES, ny), 0) % ORDER
    cbt = jnp.exp(-z_col * c_n) * pick(c_state, [poly(ORDER - 1 - a, c_n) for a in range(ORDER)])
    bent = exact(st, hat)
    own_ref[...] = hat * pass_gain

    gap = iota((ny, ny), 1) - iota((ny, ny), 0)
    z_mode = ry_ref[...] * (1.0 / extent)
    z_mode = jnp.sum(
        jnp.where(
            iota((modes, modes), 0) == iota((modes, modes), 1), jnp.broadcast_to(z_mode, (modes, modes)), 0.0
        ),
        axis=1,
        keepdims=True,
    )
    lag = iota((modes, ny), 1)
    back = jnp.where(lag == 0, 0, ny - lag).astype(F32)
    lag = lag.astype(F32)
    ahead_row = split(jnp.exp(-z_mode * lag) * poly(ORDER - 1, lag + 1.0))
    back_row = split(jnp.exp(-z_mode * back) * poly(ORDER - 1, back + 1.0))
    ahead_row = [part.astype(F32) for part in ahead_row]
    back_row = [part.astype(F32) for part in back_row]

    def band(row, inside):
        wide = jnp.broadcast_to(row, (ny, ny))
        wide = pltpu.roll(wide, 0, 1, stride=1, stride_axis=0)
        return jnp.where(inside, wide, 0.0).astype(BF16)

    group = iota((ny, LANES), 1) // ORDER
    edge = split(sbt)
    seen = jnp.zeros((ny, LANES), F32)
    for k in range(modes):
        up = [band(part[k : k + 1], gap >= 0) for part in ahead_row]
        down = [band(part[k : k + 1], gap <= 0) for part in back_row]
        both = dot3(up, [jnp.concatenate([down[i], edge[i]], 1) for i in range(2)])
        high_ref[k], low_ref[k] = split(both[:, :ny])
        seen = jnp.where(group == k, both[:, ny:], seen)

    leaving = (seen + exact(bent, moved(ny))) * (pass_gain * pass_gain)
    wide = jnp.zeros(send_ref.shape, F32)
    for d in range(1, blocks):
        ends = float(d * ny) - j
        to_right = jnp.exp(-z * (ends - 1.0)) * pick(lanes, [poly(a, ends) for a in range(ORDER)]) * pass_gain
        to_left = exact(leaving, moved((blocks - d - 1) * ny))
        chosen = jnp.where(place + d < blocks, to_right, to_left)
        pad = jnp.zeros((ny, send_ref.shape[1] - LANES), F32)
        chosen = jnp.concatenate([chosen, pad], 1) if pad.shape[1] else chosen
        wide = wide + (pltpu.roll(chosen, (d - 1) * states, 1) if d > 1 else chosen)
    send_ref[...] = wide

    flip = same & (row_state + lane_state == ORDER - 1)
    turned = exact(jnp.where(flip, jnp.exp(-z_col), 0.0), seen, ((1,), (1,)))
    bent_on = exact(exact(moved(ny), hat), cbt)
    fix = jnp.concatenate([(turned + bent_on) * (gain_col * scale_col), cbt * scale_col], 0)
    high, low = split(fix)
    fix_ref[...] = jnp.concatenate([high, low, high], 0)


def lane_group(shape, modes):
    return (iota(shape, len(shape) - 1) % (modes * ORDER)) // ORDER


def by_mode(f_ref, z_ref, members, modes, nx):
    for k in range(modes):
        for m in range(members):
            f_ref[pl.ds((k * members + m) * nx, nx), :] = z_ref[
                pl.ds(m * modes + k, nx, stride=members * modes), :
            ]


def early_kernel(extent, z_ref, send_ref, rx_ref, pre_ref, react_ref, f_ref, y_ref, w_ref):
    modes = rx_ref.shape[1]
    nx = react_ref.shape[0] // (2 * ORDER)
    rows = z_ref.shape[0] // nx
    members = rows // modes
    lines = members * nx
    lanes = send_ref.shape[1]
    by_mode(f_ref, z_ref, members, modes, nx)
    wide = dot3(split(f_ref[...]), split(send_ref[...]))
    group = lane_group((lines, lanes), modes)
    total = jnp.zeros(group.shape, F32)
    for k in range(modes):
        total = jnp.where(group == k, wide[k * lines : (k + 1) * lines], total)
    pre_ref[...] = total

    full = (2 * ORDER, lanes)
    spread = (lane_group((modes, lanes), modes) == iota((modes, lanes), 0)).astype(F32)
    z = exact(rx_ref[...], spread) * (1.0 / extent)
    g = gain(z)
    r = jnp.broadcast_to(jnp.exp(-z), full)
    pass_gain = jnp.broadcast_to((g * g) * (g * g), full)
    unit = iota(full, 0)
    zeros = jnp.zeros(full, F32)

    def onward(x, states):
        states = section(r, states, zeros)
        y_ref[pl.ds(pl.multiple_of(x * SUB, SUB), SUB), :] = states[-1] * pass_gain
        return states

    def backward(n, states):
        at = pl.ds(pl.multiple_of((nx - 1 - n) * SUB, SUB), SUB)
        states = section(r, states, y_ref[at, :])
        for t in range(lanes // LANES):
            w_ref[t, at, :] = states[-1][:, t * LANES : (t + 1) * LANES]
        return states

    first = tuple((unit == a).astype(F32) for a in range(ORDER))
    lax.fori_loop(0, nx, onward, first, unroll=8)
    first = tuple((unit == ORDER + a).astype(F32) for a in range(ORDER))
    lax.fori_loop(0, nx, backward, first, unroll=8)
    for a in range(2 * ORDER):
        for t in range(lanes // LANES):
            react_ref[pl.ds(a * nx, nx), t * LANES : (t + 1) * LANES] = w_ref[t, pl.ds(a, nx, stride=SUB), :]


def x_kernel(blocks, blocks_y, extent, end_ref, hat_ref, rx_ref, send_ref, pre_ref, react_ref, *refs):
    got = refs[: blocks - 1]
    enter_ref, msg_refs = refs[blocks - 1], refs[blocks:]
    rows = hat_ref.shape[0]
    modes = rx_ref.shape[1]
    members = rows // modes
    ny = end_ref.shape[1]
    nx = pre_ref.shape[0] // members
    place = lax.axis_index("gx")
    full = (rows, ny)
    z = column_of(rx_ref[...], lambda i: i % modes, rows) * (1.0 / extent)

    left, right = [], []
    for a in range(ORDER):
        e = jnp.zeros(full, F32)
        b = jnp.zeros(full, F32)
        for d in range(1, blocks):
            value = got[d - 1][pl.ds(a * rows, rows), :]
            behind = source(place, d, blocks) < place
            e = e + jnp.where(behind, value, 0.0)
            b = b + jnp.where(behind, 0.0, value)
        left.append(e)
        right.append(b)
    ends = shifted(power(z, nx), left)
    ends = [ends[a] + end_ref[pl.ds(a * rows, rows), :] for a in range(ORDER)]
    hat = hat_ref[...]
    for a in range(ORDER):
        for b in range(ORDER):
            at = a * ORDER + b
            right[a] = right[a] + hat[:, at : at + 1] * ends[b]
    enter = jnp.concatenate(left + right, 0)
    enter_ref[...] = enter

    wide = dot3(split(enter), split(send_ref[...]))
    lanes = wide.shape[1]
    row = iota((rows, lanes), 0)
    mine = row % modes == lane_group((rows, lanes), modes)
    states = modes * ORDER
    for m in range(members):
        here = mine & (row // modes == m)
        total = pre_ref[pl.ds(m * nx, nx), :]
        for a in range(2 * ORDER):
            value = jnp.where(here, wide[a * rows : (a + 1) * rows], 0.0)
            value = jnp.sum(value, axis=0, keepdims=True)
            total = total + react_ref[pl.ds(a * nx, nx), :] * value
        for d in range(blocks_y - 1):
            moved = pltpu.roll(total, lanes - d * states, 1) if d else total
            msg_refs[d][pl.ds(m * nx, nx), :] = moved[:, :LANES]


def local_kernel(extent, extent_x, proj_ref, enter_ref, high_ref, low_ref, e_ref, rx_ref, ry_ref, sent_ref, own_ref, out_ref, right_ref, y_ref, z_ref, f_ref):
    levels, modes = e_ref.shape
    members = out_ref.shape[0] // levels
    rows = members * modes
    nx = out_ref.shape[1]
    ny = proj_ref.shape[1]
    lines = members * nx
    full = (rows, ny)
    z = column_of(rx_ref[...], lambda i: i % modes, rows) * (1.0 / extent_x)
    g = gain(z)
    r = jnp.broadcast_to(jnp.exp(-z), full)
    pass_gain = jnp.broadcast_to((g * g) * (g * g), full)

    def onward(x, states):
        at = pl.ds(pl.multiple_of(x * rows, SUB), rows)
        states = section(r, states, proj_ref[at, :])
        y_ref[at, :] = states[-1] * pass_gain
        return states

    def backward(n, states):
        at = pl.ds(pl.multiple_of((nx - 1 - n) * rows, SUB), rows)
        states = section(r, states, y_ref[at, :])
        z_ref[at, :] = states[-1]
        return states

    left = tuple(enter_ref[pl.ds(a * rows, rows), :] for a in range(ORDER))
    lax.fori_loop(0, nx, onward, left, unroll=8)
    right = tuple(enter_ref[pl.ds((ORDER + a) * rows, rows), :] for a in range(ORDER))
    lax.fori_loop(0, nx, backward, right, unroll=8)

    right_ref[...] = exact(sent_ref[...], own_ref[...])
    by_mode(f_ref, z_ref, members, modes, nx)
    for k in range(modes):
        at = pl.ds(k * lines, lines)
        f_ref[at, :] = dot3(split(f_ref[at, :]), (high_ref[k], low_ref[k]))
    g = gain(ry_ref[...] * (1.0 / extent))
    gx = gain(rx_ref[...] * (1.0 / extent_x))
    pass_gain = (g * g) * (g * g)
    scale = jnp.sqrt((2.0 - g) / g) * jnp.sqrt((2.0 - gx) / gx) * pass_gain * pass_gain
    mix = split(expanded(e_ref[...] * scale, levels, modes))
    for t in range(nx // SUB):
        wide = jnp.concatenate(
            [
                jnp.concatenate(
                    [f_ref[pl.ds(k * lines + m * nx + t * SUB, SUB), :] for k in range(modes)], 0
                )
                for m in range(members)
            ],
            1,
        )
        done = dot3(mix, split(wide))
        for m in range(members):
            for l in range(levels):
                out_ref[m * levels + l, pl.ds(t * SUB, SUB), :] = done[
                    l * SUB : (l + 1) * SUB, m * ny : (m + 1) * ny
                ]


def final_kernel(blocks, total_members, first, p_ref, base_ref, right_ref, fix_ref, lift_ref, *refs):
    got, out_ref = refs[:-1], refs[-1]
    members, levels, nx, ny = p_ref.shape
    place = lax.axis_index("gy")
    left = jnp.zeros(got[0].shape, F32)
    right = right_ref[...]
    for d in range(1, blocks):
        value = got[d - 1][...]
        left = left + jnp.where(place >= d, value, 0.0)
        right = right + jnp.where(place >= d, 0.0, value)
    enter = jnp.concatenate([left, right], 1)
    fix = fix_ref[...]
    share = 1.0 / (total_members - 1)
    for l in range(first, first + out_ref.shape[0]):
        high, low = split(enter * lift_ref[pl.ds(l, 1), :])
        add = dot(jnp.concatenate([high, high, low], 1), fix)
        out = jnp.zeros((nx, ny), F32)
        for m in range(members):
            out = out + p_ref[m, l].astype(F32) * (
                base_ref[m * levels + l] + add[m * nx : (m + 1) * nx]
            )
        out_ref[l - first] = out * share


def call(kernel, out, ins, scratch=(), far=False, flops=0):
    spec = lambda: pl.BlockSpec(memory_space=pltpu.HBM if far else VMEM)
    nbytes = sum(a.size * a.dtype.itemsize for a in ins) + sum(
        a.size * a.dtype.itemsize for a in jax.tree.leaves(out)
    )
    return pl.pallas_call(
        kernel,
        out_shape=out,
        in_specs=[spec() for _ in range(len(ins))],
        out_specs=jax.tree.map(lambda _: pl.BlockSpec(memory_space=VMEM), out),
        scratch_shapes=list(scratch),
        cost_estimate=pl.CostEstimate(flops=flops, bytes_accessed=nbytes, transcendentals=0),
        compiler_params=pltpu.CompilerParams(vmem_limit_bytes=GRANT),
    )(*ins)


def shape(*dims):
    return jax.ShapeDtypeStruct(dims, F32)


def exchange(values, axis, to):
    n = lax.axis_size(axis)
    got = []
    for d in range(1, n):
        got.append(lax.ppermute(values[d - 1], axis, [(i, to(i, d, n)) for i in range(n)]))
    return got


def body(perturb, gradient, vertical_eigenmodes, rate_x, rate_y):
    members, levels, nx, ny = perturb.shape
    modes = vertical_eigenmodes.shape[1]
    rows = members * modes
    blocks_x, blocks_y = lax.axis_size("gx"), lax.axis_size("gy")
    extent_x, extent_y = nx * blocks_x, ny * blocks_y

    field = shape(rows * nx, ny)
    pitch = (nx // SUB | 1) * SUB
    proj, alone, ends, hat, eigen, row_x, row_y, *messages = call(
        functools.partial(project_kernel, blocks_x, extent_x),
        tuple(
            [field, field, shape(ORDER * rows, ny), shape(rows, LANES)]
            + [shape(levels, modes), shape(1, modes), shape(1, modes)]
            + [shape(ORDER * rows, ny)] * (blocks_x - 1)
        ),
        tuple(
            pltpu.with_memory_space_constraint(a, pltpu.HBM)
            for a in (perturb, gradient, vertical_eigenmodes, rate_x[None, :], rate_y[None, :])
        ),
        scratch=(
            VMEM(perturb.shape, perturb.dtype),
            VMEM(gradient.shape, F32),
            VMEM((modes * SUB, 3 * levels * SUB), BF16),
            VMEM((rows * pitch, ny), F32),
            VMEM((rows * nx, ny), F32),
            pltpu.SemaphoreType.DMA((5,)),
        ),
        far=True,
        flops=1 << 28,
    )
    got = exchange(messages, "gx", target)
    packed = -(-(blocks_y - 1) * modes * ORDER // LANES) * LANES
    half = jax.ShapeDtypeStruct((modes, ny, ny), BF16)
    send, high, low, fix, lift, own = call(
        functools.partial(table_kernel, blocks_y, extent_y, extent_x),
        (
            shape(ny, packed),
            half,
            half,
            jax.ShapeDtypeStruct((6 * LANES, ny), BF16),
            shape(levels, 2 * LANES),
            shape(LANES, LANES),
        ),
        (eigen, row_x, row_y),
        flops=1 << 30,
    )
    before, react = call(
        functools.partial(early_kernel, extent_x),
        (shape(members * nx, packed), shape(2 * ORDER * nx, packed)),
        (alone, send, row_x),
        scratch=(
            VMEM((rows * nx, ny), F32),
            VMEM((SUB * nx, packed), F32),
            VMEM((packed // LANES, SUB * nx, LANES), F32),
        ),
        flops=1 << 29,
    )
    enter, *sent = call(
        functools.partial(x_kernel, blocks_x, blocks_y, extent_x),
        tuple([shape(2 * ORDER * rows, ny)] + [shape(members * nx, LANES)] * (blocks_y - 1)),
        (ends, hat, row_x, send, before, react, *got),
        flops=1 << 27,
    )
    got = exchange(sent, "gy", lambda i, d, n: (i + d) % n)
    base, right = call(
        functools.partial(local_kernel, extent_y, extent_x),
        (shape(members * levels, nx, ny), shape(members * nx, LANES)),
        (proj, enter, high, low, eigen, row_x, row_y, sent[0], own),
        scratch=(VMEM((rows * nx, ny), F32),) * 3,
        flops=1 << 29,
    )
    pieces = 4 if levels % 4 == 0 else 1
    size = levels // pieces
    parts = [
        call(
            functools.partial(final_kernel, blocks_y, members * lax.axis_size("member"), i * size),
            shape(size, nx, ny),
            (perturb, base, right, fix, lift, *got),
            flops=1 << 27,
        )
        for i in range(pieces)
    ]
    if lax.axis_size("member") > 2:
        return lax.psum(jnp.concatenate(parts, 0), "member")
    others = [lax.ppermute(part, "member", [(0, 1), (1, 0)]) for part in parts]
    return jnp.concatenate([a + b for a, b in zip(parts, others)], 0)


def solution(mesh):
    return jax.shard_map(
        body,
        mesh=mesh,
        in_specs=(P("member", None, "gx", "gy"), P(None, "gx", "gy"), P(), P(), P()),
        out_specs=P(None, "gx", "gy"),
        check_vma=False,
    )
```

```python
import functools

import jax
import jax.numpy as jnp
from jax import lax
from jax.experimental import pallas as pl
from jax.experimental.pallas import tpu as pltpu
from jax.sharding import PartitionSpec as P

F32 = jnp.float32
BF16 = jnp.bfloat16
VMEM = pltpu.VMEM
ORDER = 4
LANES = 128
SUB = 8
GRANT = 12 << 20


def poly(d, n):
    if d == 0:
        return jnp.ones_like(n) if hasattr(n, "shape") else 1.0
    if d == 1:
        return n
    if d == 2:
        return n * (n + 1.0) * 0.5
    return n * (n + 1.0) * (n + 2.0) * (1.0 / 6.0)


def gain(z):
    series = jnp.ones_like(z)
    for k in range(12, 1, -1):
        series = 1.0 - z * series * (1.0 / k)
    return jnp.where(z < 1.0, z * series, 1.0 - jnp.exp(-z))


def split(a):
    high = a.astype(BF16)
    return high, (a - high.astype(F32)).astype(BF16)


def dot(a, b):
    return jnp.dot(a, b, preferred_element_type=F32)


def dot3(a, b):
    return dot(jnp.concatenate([a[0], a[0], a[1]], 1), jnp.concatenate([b[0], b[1], b[0]], 0))


def exact(a, b, contract=((1,), (0,))):
    return lax.dot_general(
        a, b, (contract, ((), ())), precision=lax.Precision.HIGHEST, preferred_element_type=F32
    )


def iota(shape, axis):
    return lax.broadcasted_iota(jnp.int32, shape, axis)


def column_of(row, pick, rows):
    n = row.shape[1]
    wide = jnp.broadcast_to(row, (rows, n))
    hit = iota((rows, n), 1) == pick(iota((rows, n), 0))
    return jnp.sum(jnp.where(hit, wide, 0.0), axis=1, keepdims=True)


def expanded(matrix, rows, cols):
    left = (iota((rows * SUB, rows), 0) // SUB == iota((rows * SUB, rows), 1)).astype(BF16)
    right = (iota((cols, cols * SUB), 1) // SUB == iota((cols, cols * SUB), 0)).astype(BF16)
    shape = (rows * SUB, cols * SUB)
    own = iota(shape, 0) % SUB == iota(shape, 1) % SUB
    return [
        jnp.where(own, dot(dot(left, part).astype(BF16), right), 0.0).astype(BF16)
        for part in split(matrix)
    ]


def shifted(coefficients, states):
    out = []
    for a in range(ORDER):
        total = coefficients[0] * states[a]
        for c in range(a):
            total = total + coefficients[a - c] * states[c]
        out.append(total)
    return out


def power(z, steps):
    decay = jnp.exp(-z * float(steps))
    return [decay * poly(d, float(steps)) for d in range(ORDER)]


def target(place, d, blocks):
    if blocks & (blocks - 1) == 0:
        return place ^ d
    return (place + d) % blocks


def source(place, d, blocks):
    if blocks & (blocks - 1) == 0:
        return place ^ d
    return (place - d + blocks) % blocks


def section(r, states, value):
    out = []
    for s in states:
        value = r * s + value
        out.append(value)
    return tuple(out)


def project_kernel(blocks, extent, p_hbm, g_hbm, e_hbm, rx_hbm, ry_hbm, proj_ref, z_ref, end_ref, hat_ref, e_ref, rx_ref, ry_ref, *refs):
    msg_refs = refs[: blocks - 1]
    p_ref, g_ref, mix_ref, n_ref, y_ref, sems = refs[blocks - 1 :]
    members, levels, nx, ny = p_ref.shape
    modes = e_ref.shape[1]
    rows = members * modes
    place = lax.axis_index("gx")
    depth = 2 * SUB if nx % (2 * SUB) == 0 else SUB
    pairs = [(e_hbm, e_ref), (rx_hbm, rx_ref), (ry_hbm, ry_ref), (g_hbm, g_ref), (p_hbm, p_ref)]
    copies = [pltpu.make_async_copy(a, b, sems.at[i]) for i, (a, b) in enumerate(pairs)]
    for copy in copies:
        copy.start()
    for copy in copies[:3]:
        copy.wait()
    rate = rx_ref[...]
    pitch = n_ref.shape[0] // rows

    g_rows = gain(column_of(rate, lambda i: i, modes) * (1.0 / extent))
    mix = expanded(e_ref[...].T * ((g_rows * g_rows) * (g_rows * g_rows)), modes, levels)
    mix_ref[...] = jnp.concatenate([mix[0], mix[0], mix[1]], 1)

    z = column_of(rate, lambda i: i % modes, rows) * (1.0 / extent)
    g = gain(z)
    full = (rows, ny)
    r = jnp.broadcast_to(jnp.exp(-z), full)
    pass_gain = jnp.broadcast_to((g * g) * (g * g), full)
    zeros = (jnp.zeros(full, F32),) * ORDER

    ahead = (blocks - 1 - place) * nx
    span = (blocks - 1) * nx
    span = -(-span // LANES) * LANES
    n = iota((rows, span), 1).astype(F32) + 1.0
    inside = iota((rows, span), 1) < ahead
    weight = jnp.where(inside, jnp.exp(-z * (2.0 * n - 1.0)), 0.0) * ((g * g) * (g * g))
    sums = {}
    for a in range(ORDER):
        for b in range(a, ORDER):
            sums[a, b] = jnp.sum(weight * poly(a, n) * poly(b, n), axis=1, keepdims=True)
            sums[b, a] = sums[a, b]
    hat = [[sums[a, ORDER - 1 - b] for b in range(ORDER)] for a in range(ORDER)]
    lane = iota((rows, LANES), 1)
    packed = jnp.zeros((rows, LANES), F32)
    for a in range(ORDER):
        for b in range(ORDER):
            packed = jnp.where(lane == a * ORDER + b, hat[a][b], packed)
    hat_ref[...] = packed

    for copy in copies[3:]:
        copy.wait()
    for t in range(nx // depth):
        at = pl.ds(t * depth, depth)
        parts = [
            [p_ref[m, l, at, :].astype(F32) * g_ref[l, at, :] for l in range(levels)]
            for m in range(members)
        ]
        for h in range(depth // SUB):
            wide = jnp.concatenate(
                [
                    jnp.concatenate([part[h * SUB : (h + 1) * SUB] for part in parts[m]], 0)
                    for m in range(members)
                ],
                1,
            )
            high, low = split(wide)
            done = dot(mix_ref[...], jnp.concatenate([high, low, high], 0))
            for m in range(members):
                for k in range(modes):
                    at = pl.ds((m * modes + k) * pitch + t * depth + h * SUB, SUB)
                    n_ref[at, :] = done[k * SUB : (k + 1) * SUB, m * ny : (m + 1) * ny]

    def onward(x, states):
        at = pl.ds(pl.multiple_of(x * rows, SUB), rows)
        value = n_ref[pl.ds(x, rows, stride=pitch), :]
        proj_ref[at, :] = value
        states = section(r, states, value)
        y_ref[at, :] = states[-1] * pass_gain
        return states

    def backward(n, states):
        at = pl.ds(pl.multiple_of((nx - 1 - n) * rows, SUB), rows)
        states = section(r, states, y_ref[at, :])
        z_ref[at, :] = states[-1]
        return states

    ends = lax.fori_loop(0, nx, onward, zeros, unroll=8)
    starts = lax.fori_loop(0, nx, backward, zeros, unroll=8)

    turned = [sum(hat[a][b] * ends[b] for b in range(ORDER)) for a in range(ORDER)]
    turned = shifted(power(z, nx), turned)
    leaving = [starts[a] + turned[a] for a in range(ORDER)]
    for a in range(ORDER):
        end_ref[pl.ds(a * rows, rows), :] = ends[a]
    to_right, to_left = {1: ends}, {1: leaving}
    for hops in range(2, blocks):
        over = power(z, (hops - 1) * nx)
        to_right[hops] = shifted(over, ends)
        to_left[hops] = shifted(over, leaving)
    for d in range(1, blocks):
        to = target(place, d, blocks)
        reach = sorted({abs(target(i, d, blocks) - i) for i in range(blocks)})
        for a in range(ORDER):
            value = to_right[reach[0]][a]
            for hops in reach:
                value = jnp.where(to - place == hops, to_right[hops][a], value)
                value = jnp.where(place - to == hops, to_left[hops][a], value)
            msg_refs[d - 1][pl.ds(a * rows, rows), :] = value


def table_kernel(blocks, extent, extent_x, e_ref, rx_ref, ry_ref, send_ref, high_ref, low_ref, fix_ref, lift_ref, own_ref):
    modes = e_ref.shape[1]
    ny = high_ref.shape[1]
    place = lax.axis_index("gy")
    states = modes * ORDER

    spread = (iota((modes, LANES), 1) // ORDER == iota((modes, LANES), 0)).astype(F32)
    live = (iota((1, LANES), 1) < states).astype(F32)
    lift = exact(e_ref[...], spread)
    lift_ref[...] = jnp.concatenate([lift, lift], 1)
    z = exact(ry_ref[...], spread) * (1.0 / extent)
    zx = exact(rx_ref[...], spread) * (1.0 / extent_x)
    g = gain(z)
    gx = gain(zx)
    pass_gain = (g * g) * (g * g) * live
    scale = jnp.sqrt((2.0 - g) / jnp.where(live > 0, g, 1.0)) * jnp.sqrt(
        (2.0 - gx) / jnp.where(live > 0, gx, 1.0)
    )
    scale = scale * live
    square = (LANES, LANES)
    eye = iota(square, 0) == iota(square, 1)

    def to_column(row):
        return jnp.sum(jnp.where(eye, jnp.broadcast_to(row, square), 0.0), axis=1, keepdims=True)

    def pick(index, choices):
        out = choices[0]
        for k in range(1, len(choices)):
            out = jnp.where(index == k, choices[k], out)
        return out

    z_col = to_column(z)
    scale_col = to_column(scale)
    gain_col = to_column(pass_gain)
    same = iota(square, 0) // ORDER == iota(square, 1) // ORDER
    row_state = iota(square, 0) % ORDER
    lane_state = iota(square, 1) % ORDER

    def moved(steps):
        if steps == 0:
            return jnp.where(eye, 1.0, 0.0)
        decay = jnp.exp(-z * float(steps))
        up = lane_state - row_state
        by = pick(up, [poly(d, float(steps)) for d in range(ORDER)])
        return jnp.where(same & (up >= 0), decay * by, 0.0)

    ahead = (blocks - 1 - place) * ny
    span = (blocks - 1) * ny
    n = iota((LANES, span), 1).astype(F32) + 1.0
    state = iota((LANES, span), 0) % ORDER
    inside = iota((LANES, span), 1) < ahead
    polys = [poly(d, n) for d in range(ORDER)]
    first = jnp.where(inside, jnp.exp(-z_col * n), 0.0) * pick(state, polys[::-1])
    second = jnp.exp(-z_col * (n - 1.0)) * pick(state, polys)
    hat = jnp.where(same, exact(first, second, ((1,), (1,))), 0.0)

    j = iota((ny, LANES), 0).astype(F32)
    lanes = iota((ny, LANES), 1) % ORDER
    from_end = float(ny) - j
    st = jnp.exp(-z * (from_end - 1.0)) * pick(lanes, [poly(a, from_end) for a in range(ORDER)]) * live
    sbt = jnp.exp(-z * j) * pick(lanes, [poly(a, j + 1.0) for a in range(ORDER)]) * live
    c_n = float(ny) - iota((LANES, ny), 1).astype(F32)
    c_state = iota((LANES, ny), 0) % ORDER
    cbt = jnp.exp(-z_col * c_n) * pick(c_state, [poly(ORDER - 1 - a, c_n) for a in range(ORDER)])
    bent = exact(st, hat)
    own_ref[...] = hat * pass_gain

    gap = iota((ny, ny), 1) - iota((ny, ny), 0)
    z_mode = ry_ref[...] * (1.0 / extent)
    z_mode = jnp.sum(
        jnp.where(
            iota((modes, modes), 0) == iota((modes, modes), 1), jnp.broadcast_to(z_mode, (modes, modes)), 0.0
        ),
        axis=1,
        keepdims=True,
    )
    lag = iota((modes, ny), 1)
    back = jnp.where(lag == 0, 0, ny - lag).astype(F32)
    lag = lag.astype(F32)
    ahead_row = split(jnp.exp(-z_mode * lag) * poly(ORDER - 1, lag + 1.0))
    back_row = split(jnp.exp(-z_mode * back) * poly(ORDER - 1, back + 1.0))
    ahead_row = [part.astype(F32) for part in ahead_row]
    back_row = [part.astype(F32) for part in back_row]

    def band(row, inside):
        wide = jnp.broadcast_to(row, (ny, ny))
        wide = pltpu.roll(wide, 0, 1, stride=1, stride_axis=0)
        return jnp.where(inside, wide, 0.0).astype(BF16)

    group = iota((ny, LANES), 1) // ORDER
    edge = split(sbt)
    seen = jnp.zeros((ny, LANES), F32)
    for k in range(modes):
        up = [band(part[k : k + 1], gap >= 0) for part in ahead_row]
        down = [band(part[k : k + 1], gap <= 0) for part in back_row]
        both = dot3(up, [jnp.concatenate([down[i], edge[i]], 1) for i in range(2)])
        high_ref[k], low_ref[k] = split(both[:, :ny])
        seen = jnp.where(group == k, both[:, ny:], seen)

    leaving = (seen + exact(bent, moved(ny))) * (pass_gain * pass_gain)
    wide = jnp.zeros(send_ref.shape, F32)
    for d in range(1, blocks):
        ends = float(d * ny) - j
        to_right = jnp.exp(-z * (ends - 1.0)) * pick(lanes, [poly(a, ends) for a in range(ORDER)]) * pass_gain
        to_left = exact(leaving, moved((blocks - d - 1) * ny))
        chosen = jnp.where(place + d < blocks, to_right, to_left)
        pad = jnp.zeros((ny, send_ref.shape[1] - LANES), F32)
        chosen = jnp.concatenate([chosen, pad], 1) if pad.shape[1] else chosen
        wide = wide + (pltpu.roll(chosen, (d - 1) * states, 1) if d > 1 else chosen)
    send_ref[...] = wide

    flip = same & (row_state + lane_state == ORDER - 1)
    turned = exact(jnp.where(flip, jnp.exp(-z_col), 0.0), seen, ((1,), (1,)))
    bent_on = exact(exact(moved(ny), hat), cbt)
    fix = jnp.concatenate([(turned + bent_on) * (gain_col * scale_col), cbt * scale_col], 0)
    high, low = split(fix)
    fix_ref[...] = jnp.concatenate([high, low, high], 0)


def lane_group(shape, modes):
    return (iota(shape, len(shape) - 1) % (modes * ORDER)) // ORDER


def by_mode(f_ref, z_ref, members, modes, nx):
    for k in range(modes):
        for m in range(members):
            f_ref[pl.ds((k * members + m) * nx, nx), :] = z_ref[
                pl.ds(m * modes + k, nx, stride=members * modes), :
            ]


def early_kernel(extent, z_ref, send_ref, rx_ref, pre_ref, react_ref, f_ref, y_ref, w_ref):
    modes = rx_ref.shape[1]
    nx = react_ref.shape[0] // (2 * ORDER)
    rows = z_ref.shape[0] // nx
    members = rows // modes
    lines = members * nx
    lanes = send_ref.shape[1]
    by_mode(f_ref, z_ref, members, modes, nx)
    wide = dot3(split(f_ref[...]), split(send_ref[...]))
    group = lane_group((lines, lanes), modes)
    total = jnp.zeros(group.shape, F32)
    for k in range(modes):
        total = jnp.where(group == k, wide[k * lines : (k + 1) * lines], total)
    pre_ref[...] = total

    full = (2 * ORDER, lanes)
    spread = (lane_group((modes, lanes), modes) == iota((modes, lanes), 0)).astype(F32)
    z = exact(rx_ref[...], spread) * (1.0 / extent)
    g = gain(z)
    r = jnp.broadcast_to(jnp.exp(-z), full)
    pass_gain = jnp.broadcast_to((g * g) * (g * g), full)
    unit = iota(full, 0)
    zeros = jnp.zeros(full, F32)

    def onward(x, states):
        states = section(r, states, zeros)
        y_ref[pl.ds(pl.multiple_of(x * SUB, SUB), SUB), :] = states[-1] * pass_gain
        return states

    def backward(n, states):
        at = pl.ds(pl.multiple_of((nx - 1 - n) * SUB, SUB), SUB)
        states = section(r, states, y_ref[at, :])
        for t in range(lanes // LANES):
            w_ref[t, at, :] = states[-1][:, t * LANES : (t + 1) * LANES]
        return states

    first = tuple((unit == a).astype(F32) for a in range(ORDER))
    lax.fori_loop(0, nx, onward, first, unroll=8)
    first = tuple((unit == ORDER + a).astype(F32) for a in range(ORDER))
    lax.fori_loop(0, nx, backward, first, unroll=8)
    for a in range(2 * ORDER):
        for t in range(lanes // LANES):
            react_ref[pl.ds(a * nx, nx), t * LANES : (t + 1) * LANES] = w_ref[t, pl.ds(a, nx, stride=SUB), :]


def x_kernel(blocks, blocks_y, extent, end_ref, hat_ref, rx_ref, send_ref, pre_ref, react_ref, *refs):
    got = refs[: blocks - 1]
    enter_ref, msg_refs = refs[blocks - 1], refs[blocks:]
    rows = hat_ref.shape[0]
    modes = rx_ref.shape[1]
    members = rows // modes
    ny = end_ref.shape[1]
    nx = pre_ref.shape[0] // members
    place = lax.axis_index("gx")
    full = (rows, ny)
    z = column_of(rx_ref[...], lambda i: i % modes, rows) * (1.0 / extent)

    left, right = [], []
    for a in range(ORDER):
        e = jnp.zeros(full, F32)
        b = jnp.zeros(full, F32)
        for d in range(1, blocks):
            value = got[d - 1][pl.ds(a * rows, rows), :]
            behind = source(place, d, blocks) < place
            e = e + jnp.where(behind, value, 0.0)
            b = b + jnp.where(behind, 0.0, value)
        left.append(e)
        right.append(b)
    ends = shifted(power(z, nx), left)
    ends = [ends[a] + end_ref[pl.ds(a * rows, rows), :] for a in range(ORDER)]
    hat = hat_ref[...]
    for a in range(ORDER):
        for b in range(ORDER):
            at = a * ORDER + b
            right[a] = right[a] + hat[:, at : at + 1] * ends[b]
    enter = jnp.concatenate(left + right, 0)
    enter_ref[...] = enter

    wide = dot3(split(enter), split(send_ref[...]))
    lanes = wide.shape[1]
    row = iota((rows, lanes), 0)
    mine = row % modes == lane_group((rows, lanes), modes)
    states = modes * ORDER
    for m in range(members):
        here = mine & (row // modes == m)
        total = pre_ref[pl.ds(m * nx, nx), :]
        for a in range(2 * ORDER):
            value = jnp.where(here, wide[a * rows : (a + 1) * rows], 0.0)
            value = jnp.sum(value, axis=0, keepdims=True)
            total = total + react_ref[pl.ds(a * nx, nx), :] * value
        for d in range(blocks_y - 1):
            moved = pltpu.roll(total, lanes - d * states, 1) if d else total
            msg_refs[d][pl.ds(m * nx, nx), :] = moved[:, :LANES]


def local_kernel(extent, extent_x, proj_ref, enter_ref, high_ref, low_ref, e_ref, rx_ref, ry_ref, sent_ref, own_ref, out_ref, right_ref, y_ref, z_ref, f_ref):
    levels, modes = e_ref.shape
    members = out_ref.shape[0] // levels
    rows = members * modes
    nx = out_ref.shape[1]
    ny = proj_ref.shape[1]
    lines = members * nx
    full = (rows, ny)
    z = column_of(rx_ref[...], lambda i: i % modes, rows) * (1.0 / extent_x)
    g = gain(z)
    r = jnp.broadcast_to(jnp.exp(-z), full)
    pass_gain = jnp.broadcast_to((g * g) * (g * g), full)

    def onward(x, states):
        at = pl.ds(pl.multiple_of(x * rows, SUB), rows)
        states = section(r, states, proj_ref[at, :])
        y_ref[at, :] = states[-1] * pass_gain
        return states

    def backward(n, states):
        at = pl.ds(pl.multiple_of((nx - 1 - n) * rows, SUB), rows)
        states = section(r, states, y_ref[at, :])
        z_ref[at, :] = states[-1]
        return states

    left = tuple(enter_ref[pl.ds(a * rows, rows), :] for a in range(ORDER))
    lax.fori_loop(0, nx, onward, left, unroll=8)
    right = tuple(enter_ref[pl.ds((ORDER + a) * rows, rows), :] for a in range(ORDER))
    lax.fori_loop(0, nx, backward, right, unroll=8)

    right_ref[...] = exact(sent_ref[...], own_ref[...])
    by_mode(f_ref, z_ref, members, modes, nx)
    for k in range(modes):
        at = pl.ds(k * lines, lines)
        f_ref[at, :] = dot3(split(f_ref[at, :]), (high_ref[k], low_ref[k]))
    g = gain(ry_ref[...] * (1.0 / extent))
    gx = gain(rx_ref[...] * (1.0 / extent_x))
    pass_gain = (g * g) * (g * g)
    scale = jnp.sqrt((2.0 - g) / g) * jnp.sqrt((2.0 - gx) / gx) * pass_gain * pass_gain
    mix = expanded(e_ref[...] * scale, levels, modes)
    for t in range(nx // SUB):
        wide = jnp.concatenate(
            [
                jnp.concatenate(
                    [f_ref[pl.ds(k * lines + m * nx + t * SUB, SUB), :] for k in range(modes)], 0
                )
                for m in range(members)
            ],
            1,
        )
        done = dot3(mix, split(wide))
        for m in range(members):
            for l in range(levels):
                out_ref[m * levels + l, pl.ds(t * SUB, SUB), :] = done[
                    l * SUB : (l + 1) * SUB, m * ny : (m + 1) * ny
                ]


def final_kernel(blocks, total_members, first, p_ref, base_ref, right_ref, fix_ref, lift_ref, *refs):
    got, out_ref = refs[:-1], refs[-1]
    members, levels, nx, ny = p_ref.shape
    place = lax.axis_index("gy")
    left = jnp.zeros(got[0].shape, F32)
    right = right_ref[...]
    for d in range(1, blocks):
        value = got[d - 1][...]
        left = left + jnp.where(place >= d, value, 0.0)
        right = right + jnp.where(place >= d, 0.0, value)
    enter = jnp.concatenate([left, right], 1)
    fix = fix_ref[...]
    share = 1.0 / (total_members - 1)
    for l in range(first, first + out_ref.shape[0]):
        high, low = split(enter * lift_ref[pl.ds(l, 1), :])
        add = dot(jnp.concatenate([high, high, low], 1), fix)
        out = jnp.zeros((nx, ny), F32)
        for m in range(members):
            out = out + p_ref[m, l].astype(F32) * (
                base_ref[m * levels + l] + add[m * nx : (m + 1) * nx]
            )
        out_ref[l - first] = out * share


def call(kernel, out, ins, scratch=(), far=False, flops=0):
    spec = lambda: pl.BlockSpec(memory_space=pltpu.HBM if far else VMEM)
    nbytes = sum(a.size * a.dtype.itemsize for a in ins) + sum(
        a.size * a.dtype.itemsize for a in jax.tree.leaves(out)
    )
    return pl.pallas_call(
        kernel,
        out_shape=out,
        in_specs=[spec() for _ in range(len(ins))],
        out_specs=jax.tree.map(lambda _: pl.BlockSpec(memory_space=VMEM), out),
        scratch_shapes=list(scratch),
        cost_estimate=pl.CostEstimate(flops=flops, bytes_accessed=nbytes, transcendentals=0),
        compiler_params=pltpu.CompilerParams(vmem_limit_bytes=GRANT),
    )(*ins)


def shape(*dims):
    return jax.ShapeDtypeStruct(dims, F32)


def exchange(values, axis, to):
    n = lax.axis_size(axis)
    got = []
    for d in range(1, n):
        got.append(lax.ppermute(values[d - 1], axis, [(i, to(i, d, n)) for i in range(n)]))
    return got


def body(perturb, gradient, vertical_eigenmodes, rate_x, rate_y):
    members, levels, nx, ny = perturb.shape
    modes = vertical_eigenmodes.shape[1]
    rows = members * modes
    blocks_x, blocks_y = lax.axis_size("gx"), lax.axis_size("gy")
    extent_x, extent_y = nx * blocks_x, ny * blocks_y

    field = shape(rows * nx, ny)
    pitch = (nx // SUB | 1) * SUB
    proj, alone, ends, hat, eigen, row_x, row_y, *messages = call(
        functools.partial(project_kernel, blocks_x, extent_x),
        tuple(
            [field, field, shape(ORDER * rows, ny), shape(rows, LANES)]
            + [shape(levels, modes), shape(1, modes), shape(1, modes)]
            + [shape(ORDER * rows, ny)] * (blocks_x - 1)
        ),
        tuple(
            pltpu.with_memory_space_constraint(a, pltpu.HBM)
            for a in (perturb, gradient, vertical_eigenmodes, rate_x[None, :], rate_y[None, :])
        ),
        scratch=(
            VMEM(perturb.shape, perturb.dtype),
            VMEM(gradient.shape, F32),
            VMEM((modes * SUB, 3 * levels * SUB), BF16),
            VMEM((rows * pitch, ny), F32),
            VMEM((rows * nx, ny), F32),
            pltpu.SemaphoreType.DMA((5,)),
        ),
        far=True,
        flops=1 << 28,
    )
    got = exchange(messages, "gx", target)
    packed = -(-(blocks_y - 1) * modes * ORDER // LANES) * LANES
    half = jax.ShapeDtypeStruct((modes, ny, ny), BF16)
    send, high, low, fix, lift, own = call(
        functools.partial(table_kernel, blocks_y, extent_y, extent_x),
        (
            shape(ny, packed),
            half,
            half,
            jax.ShapeDtypeStruct((6 * LANES, ny), BF16),
            shape(levels, 2 * LANES),
            shape(LANES, LANES),
        ),
        (eigen, row_x, row_y),
        flops=1 << 30,
    )
    before, react = call(
        functools.partial(early_kernel, extent_x),
        (shape(members * nx, packed), shape(2 * ORDER * nx, packed)),
        (alone, send, row_x),
        scratch=(
            VMEM((rows * nx, ny), F32),
            VMEM((SUB * nx, packed), F32),
            VMEM((packed // LANES, SUB * nx, LANES), F32),
        ),
        flops=1 << 29,
    )
    enter, *sent = call(
        functools.partial(x_kernel, blocks_x, blocks_y, extent_x),
        tuple([shape(2 * ORDER * rows, ny)] + [shape(members * nx, LANES)] * (blocks_y - 1)),
        (ends, hat, row_x, send, before, react, *got),
        flops=1 << 27,
    )
    got = exchange(sent, "gy", lambda i, d, n: (i + d) % n)
    base, right = call(
        functools.partial(local_kernel, extent_y, extent_x),
        (shape(members * levels, nx, ny), shape(members * nx, LANES)),
        (proj, enter, high, low, eigen, row_x, row_y, sent[0], own),
        scratch=(VMEM((rows * nx, ny), F32),) * 3,
        flops=1 << 29,
    )
    pieces = 4 if levels % 4 == 0 else 1
    size = levels // pieces
    parts = [
        call(
            functools.partial(final_kernel, blocks_y, members * lax.axis_size("member"), i * size),
            shape(size, nx, ny),
            (perturb, base, right, fix, lift, *got),
            flops=1 << 27,
        )
        for i in range(pieces)
    ]
    if lax.axis_size("member") > 2:
        return lax.psum(jnp.concatenate(parts, 0), "member")
    others = [lax.ppermute(part, "member", [(0, 1), (1, 0)]) for part in parts]
    return jnp.concatenate([a + b for a, b in zip(parts, others)], 0)


def solution(mesh):
    return jax.shard_map(
        body,
        mesh=mesh,
        in_specs=(P("member", None, "gx", "gy"), P(None, "gx", "gy"), P(), P(), P()),
        out_specs=P(None, "gx", "gy"),
        check_vma=False,
    )
```

```python
import functools

import jax
import jax.numpy as jnp
from jax import lax
from jax.experimental import pallas as pl
from jax.experimental.pallas import tpu as pltpu
from jax.sharding import PartitionSpec as P

F32 = jnp.float32
BF16 = jnp.bfloat16
VMEM = pltpu.VMEM
ORDER = 4
LANES = 128
SUB = 8
GRANT = 12 << 20


def poly(d, n):
    if d == 0:
        return jnp.ones_like(n) if hasattr(n, "shape") else 1.0
    if d == 1:
        return n
    if d == 2:
        return n * (n + 1.0) * 0.5
    return n * (n + 1.0) * (n + 2.0) * (1.0 / 6.0)


def gain(z):
    series = jnp.ones_like(z)
    for k in range(12, 1, -1):
        series = 1.0 - z * series * (1.0 / k)
    return jnp.where(z < 1.0, z * series, 1.0 - jnp.exp(-z))


def split(a):
    high = a.astype(BF16)
    return high, (a - high.astype(F32)).astype(BF16)


def dot(a, b):
    return jnp.dot(a, b, preferred_element_type=F32)


def dot3(a, b):
    return dot(jnp.concatenate([a[0], a[0], a[1]], 1), jnp.concatenate([b[0], b[1], b[0]], 0))


def exact(a, b, contract=((1,), (0,))):
    return lax.dot_general(
        a, b, (contract, ((), ())), precision=lax.Precision.HIGHEST, preferred_element_type=F32
    )


def iota(shape, axis):
    return lax.broadcasted_iota(jnp.int32, shape, axis)


def column_of(row, pick, rows):
    n = row.shape[1]
    wide = jnp.broadcast_to(row, (rows, n))
    hit = iota((rows, n), 1) == pick(iota((rows, n), 0))
    return jnp.sum(jnp.where(hit, wide, 0.0), axis=1, keepdims=True)


def expanded(matrix, rows, cols):
    left = (iota((rows * SUB, rows), 0) // SUB == iota((rows * SUB, rows), 1)).astype(BF16)
    right = (iota((cols, cols * SUB), 1) // SUB == iota((cols, cols * SUB), 0)).astype(BF16)
    shape = (rows * SUB, cols * SUB)
    own = iota(shape, 0) % SUB == iota(shape, 1) % SUB
    return [
        jnp.where(own, dot(dot(left, part).astype(BF16), right), 0.0).astype(BF16)
        for part in split(matrix)
    ]


def shifted(coefficients, states):
    out = []
    for a in range(ORDER):
        total = coefficients[0] * states[a]
        for c in range(a):
            total = total + coefficients[a - c] * states[c]
        out.append(total)
    return out


def power(z, steps):
    decay = jnp.exp(-z * float(steps))
    return [decay * poly(d, float(steps)) for d in range(ORDER)]


def target(place, d, blocks):
    if blocks & (blocks - 1) == 0:
        return place ^ d
    return (place + d) % blocks


def source(place, d, blocks):
    if blocks & (blocks - 1) == 0:
        return place ^ d
    return (place - d + blocks) % blocks


def section(r, states, value):
    out = []
    for s in states:
        value = r * s + value
        out.append(value)
    return tuple(out)


def project_kernel(blocks, extent, p_hbm, g_hbm, e_hbm, rx_hbm, ry_hbm, proj_ref, z_ref, end_ref, hat_ref, e_ref, rx_ref, ry_ref, *refs):
    msg_refs = refs[: blocks - 1]
    p_ref, g_ref, mix_ref, n_ref, y_ref, sems = refs[blocks - 1 :]
    members, levels, nx, ny = p_ref.shape
    modes = e_ref.shape[1]
    rows = members * modes
    place = lax.axis_index("gx")
    depth = 2 * SUB if nx % (2 * SUB) == 0 else SUB
    pairs = [(e_hbm, e_ref), (rx_hbm, rx_ref), (ry_hbm, ry_ref), (g_hbm, g_ref), (p_hbm, p_ref)]
    copies = [pltpu.make_async_copy(a, b, sems.at[i]) for i, (a, b) in enumerate(pairs)]
    for copy in copies:
        copy.start()
    for copy in copies[:3]:
        copy.wait()
    rate = rx_ref[...]
    pitch = n_ref.shape[0] // rows

    g_rows = gain(column_of(rate, lambda i: i, modes) * (1.0 / extent))
    mix = expanded(e_ref[...].T * ((g_rows * g_rows) * (g_rows * g_rows)), modes, levels)
    mix_ref[...] = jnp.concatenate([mix[0], mix[0], mix[1]], 1)

    z = column_of(rate, lambda i: i % modes, rows) * (1.0 / extent)
    g = gain(z)
    full = (rows, ny)
    r = jnp.broadcast_to(jnp.exp(-z), full)
    pass_gain = jnp.broadcast_to((g * g) * (g * g), full)
    zeros = (jnp.zeros(full, F32),) * ORDER

    ahead = (blocks - 1 - place) * nx
    span = (blocks - 1) * nx
    span = -(-span // LANES) * LANES
    n = iota((rows, span), 1).astype(F32) + 1.0
    inside = iota((rows, span), 1) < ahead
    weight = jnp.where(inside, jnp.exp(-z * (2.0 * n - 1.0)), 0.0) * ((g * g) * (g * g))
    sums = {}
    for a in range(ORDER):
        for b in range(a, ORDER):
            sums[a, b] = jnp.sum(weight * poly(a, n) * poly(b, n), axis=1, keepdims=True)
            sums[b, a] = sums[a, b]
    hat = [[sums[a, ORDER - 1 - b] for b in range(ORDER)] for a in range(ORDER)]
    lane = iota((rows, LANES), 1)
    packed = jnp.zeros((rows, LANES), F32)
    for a in range(ORDER):
        for b in range(ORDER):
            packed = jnp.where(lane == a * ORDER + b, hat[a][b], packed)
    hat_ref[...] = packed
    wide_hat = [[jnp.broadcast_to(value, full) for value in line] for line in hat]
    over = {h: [jnp.broadcast_to(c, full) for c in power(z, h * nx)] for h in range(1, max(blocks - 1, 2))}

    for copy in copies[3:]:
        copy.wait()
    for t in range(nx // depth):
        at = pl.ds(t * depth, depth)
        parts = [
            [p_ref[m, l, at, :].astype(F32) * g_ref[l, at, :] for l in range(levels)]
            for m in range(members)
        ]
        for h in range(depth // SUB):
            wide = jnp.concatenate(
                [
                    jnp.concatenate([part[h * SUB : (h + 1) * SUB] for part in parts[m]], 0)
                    for m in range(members)
                ],
                1,
            )
            high, low = split(wide)
            done = dot(mix_ref[...], jnp.concatenate([high, low, high], 0))
            for m in range(members):
                for k in range(modes):
                    at = pl.ds((m * modes + k) * pitch + t * depth + h * SUB, SUB)
                    n_ref[at, :] = done[k * SUB : (k + 1) * SUB, m * ny : (m + 1) * ny]

    def onward(x, states):
        at = pl.ds(pl.multiple_of(x * rows, SUB), rows)
        value = n_ref[pl.ds(x, rows, stride=pitch), :]
        proj_ref[at, :] = value
        states = section(r, states, value)
        y_ref[at, :] = states[-1] * pass_gain
        return states

    def backward(n, states):
        at = pl.ds(pl.multiple_of((nx - 1 - n) * rows, SUB), rows)
        states = section(r, states, y_ref[at, :])
        z_ref[at, :] = states[-1]
        return states

    ends = lax.fori_loop(0, nx, onward, zeros, unroll=8)
    starts = lax.fori_loop(0, nx, backward, zeros, unroll=8)

    turned = [sum(wide_hat[a][b] * ends[b] for b in range(ORDER)) for a in range(ORDER)]
    turned = shifted(over[1], turned)
    leaving = [starts[a] + turned[a] for a in range(ORDER)]
    for a in range(ORDER):
        end_ref[pl.ds(a * rows, rows), :] = ends[a]
    to_right, to_left = {1: ends}, {1: leaving}
    for hops in range(2, blocks):
        to_right[hops] = shifted(over[hops - 1], ends)
        to_left[hops] = shifted(over[hops - 1], leaving)
    for d in range(1, blocks):
        to = target(place, d, blocks)
        reach = sorted({abs(target(i, d, blocks) - i) for i in range(blocks)})
        for a in range(ORDER):
            value = to_right[reach[0]][a]
            for hops in reach:
                value = jnp.where(to - place == hops, to_right[hops][a], value)
                value = jnp.where(place - to == hops, to_left[hops][a], value)
            msg_refs[d - 1][pl.ds(a * rows, rows), :] = value


def table_kernel(blocks, extent, extent_x, e_ref, rx_ref, ry_ref, send_ref, high_ref, low_ref, fix_ref, lift_ref, own_ref):
    modes = e_ref.shape[1]
    ny = high_ref.shape[1]
    place = lax.axis_index("gy")
    states = modes * ORDER

    spread = (iota((modes, LANES), 1) // ORDER == iota((modes, LANES), 0)).astype(F32)
    live = (iota((1, LANES), 1) < states).astype(F32)
    lift = exact(e_ref[...], spread)
    lift_ref[...] = jnp.concatenate([lift, lift], 1)
    z = exact(ry_ref[...], spread) * (1.0 / extent)
    zx = exact(rx_ref[...], spread) * (1.0 / extent_x)
    g = gain(z)
    gx = gain(zx)
    pass_gain = (g * g) * (g * g) * live
    scale = jnp.sqrt((2.0 - g) / jnp.where(live > 0, g, 1.0)) * jnp.sqrt(
        (2.0 - gx) / jnp.where(live > 0, gx, 1.0)
    )
    scale = scale * live
    square = (LANES, LANES)
    eye = iota(square, 0) == iota(square, 1)

    def to_column(row):
        return jnp.sum(jnp.where(eye, jnp.broadcast_to(row, square), 0.0), axis=1, keepdims=True)

    def pick(index, choices):
        out = choices[0]
        for k in range(1, len(choices)):
            out = jnp.where(index == k, choices[k], out)
        return out

    z_col = to_column(z)
    scale_col = to_column(scale)
    gain_col = to_column(pass_gain)
    same = iota(square, 0) // ORDER == iota(square, 1) // ORDER
    row_state = iota(square, 0) % ORDER
    lane_state = iota(square, 1) % ORDER

    def moved(steps):
        if steps == 0:
            return jnp.where(eye, 1.0, 0.0)
        decay = jnp.exp(-z * float(steps))
        up = lane_state - row_state
        by = pick(up, [poly(d, float(steps)) for d in range(ORDER)])
        return jnp.where(same & (up >= 0), decay * by, 0.0)

    ahead = (blocks - 1 - place) * ny
    span = (blocks - 1) * ny
    n = iota((LANES, span), 1).astype(F32) + 1.0
    state = iota((LANES, span), 0) % ORDER
    inside = iota((LANES, span), 1) < ahead
    polys = [poly(d, n) for d in range(ORDER)]
    first = jnp.where(inside, jnp.exp(-z_col * n), 0.0) * pick(state, polys[::-1])
    second = jnp.exp(-z_col * (n - 1.0)) * pick(state, polys)
    hat = jnp.where(same, exact(first, second, ((1,), (1,))), 0.0)

    j = iota((ny, LANES), 0).astype(F32)
    lanes = iota((ny, LANES), 1) % ORDER
    from_end = float(ny) - j
    st = jnp.exp(-z * (from_end - 1.0)) * pick(lanes, [poly(a, from_end) for a in range(ORDER)]) * live
    sbt = jnp.exp(-z * j) * pick(lanes, [poly(a, j + 1.0) for a in range(ORDER)]) * live
    c_n = float(ny) - iota((LANES, ny), 1).astype(F32)
    c_state = iota((LANES, ny), 0) % ORDER
    cbt = jnp.exp(-z_col * c_n) * pick(c_state, [poly(ORDER - 1 - a, c_n) for a in range(ORDER)])
    bent = exact(st, hat)
    own_ref[...] = hat * pass_gain

    gap = iota((ny, ny), 1) - iota((ny, ny), 0)
    z_mode = ry_ref[...] * (1.0 / extent)
    z_mode = jnp.sum(
        jnp.where(
            iota((modes, modes), 0) == iota((modes, modes), 1), jnp.broadcast_to(z_mode, (modes, modes)), 0.0
        ),
        axis=1,
        keepdims=True,
    )
    lag = iota((modes, ny), 1)
    back = jnp.where(lag == 0, 0, ny - lag).astype(F32)
    lag = lag.astype(F32)
    ahead_row = split(jnp.exp(-z_mode * lag) * poly(ORDER - 1, lag + 1.0))
    back_row = split(jnp.exp(-z_mode * back) * poly(ORDER - 1, back + 1.0))
    ahead_row = [part.astype(F32) for part in ahead_row]
    back_row = [part.astype(F32) for part in back_row]

    def band(row, inside):
        wide = jnp.broadcast_to(row, (ny, ny))
        wide = pltpu.roll(wide, 0, 1, stride=1, stride_axis=0)
        return jnp.where(inside, wide, 0.0).astype(BF16)

    group = iota((ny, LANES), 1) // ORDER
    edge = split(sbt)
    seen = jnp.zeros((ny, LANES), F32)
    for k in range(modes):
        up = [band(part[k : k + 1], gap >= 0) for part in ahead_row]
        down = [band(part[k : k + 1], gap <= 0) for part in back_row]
        both = dot3(up, [jnp.concatenate([down[i], edge[i]], 1) for i in range(2)])
        high_ref[k], low_ref[k] = split(both[:, :ny])
        seen = jnp.where(group == k, both[:, ny:], seen)

    leaving = (seen + exact(bent, moved(ny))) * (pass_gain * pass_gain)
    wide = jnp.zeros(send_ref.shape, F32)
    for d in range(1, blocks):
        ends = float(d * ny) - j
        to_right = jnp.exp(-z * (ends - 1.0)) * pick(lanes, [poly(a, ends) for a in range(ORDER)]) * pass_gain
        to_left = exact(leaving, moved((blocks - d - 1) * ny))
        chosen = jnp.where(place + d < blocks, to_right, to_left)
        pad = jnp.zeros((ny, send_ref.shape[1] - LANES), F32)
        chosen = jnp.concatenate([chosen, pad], 1) if pad.shape[1] else chosen
        wide = wide + (pltpu.roll(chosen, (d - 1) * states, 1) if d > 1 else chosen)
    send_ref[...] = wide

    flip = same & (row_state + lane_state == ORDER - 1)
    turned = exact(jnp.where(flip, jnp.exp(-z_col), 0.0), seen, ((1,), (1,)))
    bent_on = exact(exact(moved(ny), hat), cbt)
    fix = jnp.concatenate([(turned + bent_on) * (gain_col * scale_col), cbt * scale_col], 0)
    high, low = split(fix)
    fix_ref[...] = jnp.concatenate([high, low, high], 0)


def lane_group(shape, modes):
    return (iota(shape, len(shape) - 1) % (modes * ORDER)) // ORDER


def by_mode(f_ref, z_ref, members, modes, nx):
    for k in range(modes):
        for m in range(members):
            f_ref[pl.ds((k * members + m) * nx, nx), :] = z_ref[
                pl.ds(m * modes + k, nx, stride=members * modes), :
            ]


def early_kernel(extent, z_ref, send_ref, rx_ref, pre_ref, react_ref, f_ref, y_ref, w_ref):
    modes = rx_ref.shape[1]
    nx = react_ref.shape[0] // (2 * ORDER)
    rows = z_ref.shape[0] // nx
    members = rows // modes
    lines = members * nx
    lanes = send_ref.shape[1]
    by_mode(f_ref, z_ref, members, modes, nx)
    wide = dot3(split(f_ref[...]), split(send_ref[...]))
    group = lane_group((lines, lanes), modes)
    total = jnp.zeros(group.shape, F32)
    for k in range(modes):
        total = jnp.where(group == k, wide[k * lines : (k + 1) * lines], total)
    pre_ref[...] = total

    full = (2 * ORDER, lanes)
    spread = (lane_group((modes, lanes), modes) == iota((modes, lanes), 0)).astype(F32)
    z = exact(rx_ref[...], spread) * (1.0 / extent)
    g = gain(z)
    r = jnp.broadcast_to(jnp.exp(-z), full)
    pass_gain = jnp.broadcast_to((g * g) * (g * g), full)
    unit = iota(full, 0)
    zeros = jnp.zeros(full, F32)

    def onward(x, states):
        states = section(r, states, zeros)
        y_ref[pl.ds(pl.multiple_of(x * SUB, SUB), SUB), :] = states[-1] * pass_gain
        return states

    def backward(n, states):
        at = pl.ds(pl.multiple_of((nx - 1 - n) * SUB, SUB), SUB)
        states = section(r, states, y_ref[at, :])
        for t in range(lanes // LANES):
            w_ref[t, at, :] = states[-1][:, t * LANES : (t + 1) * LANES]
        return states

    first = tuple((unit == a).astype(F32) for a in range(ORDER))
    lax.fori_loop(0, nx, onward, first, unroll=8)
    first = tuple((unit == ORDER + a).astype(F32) for a in range(ORDER))
    lax.fori_loop(0, nx, backward, first, unroll=8)
    for a in range(2 * ORDER):
        for t in range(lanes // LANES):
            react_ref[pl.ds(a * nx, nx), t * LANES : (t + 1) * LANES] = w_ref[t, pl.ds(a, nx, stride=SUB), :]


def x_kernel(blocks, blocks_y, extent, end_ref, hat_ref, rx_ref, send_ref, pre_ref, react_ref, *refs):
    got = refs[: blocks - 1]
    enter_ref, msg_refs = refs[blocks - 1], refs[blocks:]
    rows = hat_ref.shape[0]
    modes = rx_ref.shape[1]
    members = rows // modes
    ny = end_ref.shape[1]
    nx = pre_ref.shape[0] // members
    place = lax.axis_index("gx")
    full = (rows, ny)
    z = column_of(rx_ref[...], lambda i: i % modes, rows) * (1.0 / extent)

    left, right = [], []
    for a in range(ORDER):
        e = jnp.zeros(full, F32)
        b = jnp.zeros(full, F32)
        for d in range(1, blocks):
            value = got[d - 1][pl.ds(a * rows, rows), :]
            behind = source(place, d, blocks) < place
            e = e + jnp.where(behind, value, 0.0)
            b = b + jnp.where(behind, 0.0, value)
        left.append(e)
        right.append(b)
    ends = shifted(power(z, nx), left)
    ends = [ends[a] + end_ref[pl.ds(a * rows, rows), :] for a in range(ORDER)]
    hat = hat_ref[...]
    for a in range(ORDER):
        for b in range(ORDER):
            at = a * ORDER + b
            right[a] = right[a] + hat[:, at : at + 1] * ends[b]
    enter = jnp.concatenate(left + right, 0)
    enter_ref[...] = enter

    wide = dot3(split(enter), split(send_ref[...]))
    lanes = wide.shape[1]
    row = iota((rows, lanes), 0)
    mine = row % modes == lane_group((rows, lanes), modes)
    states = modes * ORDER
    for m in range(members):
        here = mine & (row // modes == m)
        total = pre_ref[pl.ds(m * nx, nx), :]
        for a in range(2 * ORDER):
            value = jnp.where(here, wide[a * rows : (a + 1) * rows], 0.0)
            value = jnp.sum(value, axis=0, keepdims=True)
            total = total + react_ref[pl.ds(a * nx, nx), :] * value
        for d in range(blocks_y - 1):
            moved = pltpu.roll(total, lanes - d * states, 1) if d else total
            msg_refs[d][pl.ds(m * nx, nx), :] = moved[:, :LANES]


def local_kernel(extent, extent_x, proj_ref, enter_ref, high_ref, low_ref, e_ref, rx_ref, ry_ref, sent_ref, own_ref, out_ref, right_ref, y_ref, z_ref, f_ref):
    levels, modes = e_ref.shape
    members = out_ref.shape[0] // levels
    rows = members * modes
    nx = out_ref.shape[1]
    ny = proj_ref.shape[1]
    lines = members * nx
    full = (rows, ny)
    z = column_of(rx_ref[...], lambda i: i % modes, rows) * (1.0 / extent_x)
    g = gain(z)
    r = jnp.broadcast_to(jnp.exp(-z), full)
    pass_gain = jnp.broadcast_to((g * g) * (g * g), full)

    def onward(x, states):
        at = pl.ds(pl.multiple_of(x * rows, SUB), rows)
        states = section(r, states, proj_ref[at, :])
        y_ref[at, :] = states[-1] * pass_gain
        return states

    def backward(n, states):
        at = pl.ds(pl.multiple_of((nx - 1 - n) * rows, SUB), rows)
        states = section(r, states, y_ref[at, :])
        z_ref[at, :] = states[-1]
        return states

    left = tuple(enter_ref[pl.ds(a * rows, rows), :] for a in range(ORDER))
    lax.fori_loop(0, nx, onward, left, unroll=8)
    right = tuple(enter_ref[pl.ds((ORDER + a) * rows, rows), :] for a in range(ORDER))
    lax.fori_loop(0, nx, backward, right, unroll=8)

    right_ref[...] = exact(sent_ref[...], own_ref[...])
    by_mode(f_ref, z_ref, members, modes, nx)
    for k in range(modes):
        at = pl.ds(k * lines, lines)
        f_ref[at, :] = dot3(split(f_ref[at, :]), (high_ref[k], low_ref[k]))
    g = gain(ry_ref[...] * (1.0 / extent))
    gx = gain(rx_ref[...] * (1.0 / extent_x))
    pass_gain = (g * g) * (g * g)
    scale = jnp.sqrt((2.0 - g) / g) * jnp.sqrt((2.0 - gx) / gx) * pass_gain * pass_gain
    mix = expanded(e_ref[...] * scale, levels, modes)
    for t in range(nx // SUB):
        wide = jnp.concatenate(
            [
                jnp.concatenate(
                    [f_ref[pl.ds(k * lines + m * nx + t * SUB, SUB), :] for k in range(modes)], 0
                )
                for m in range(members)
            ],
            1,
        )
        done = dot3(mix, split(wide))
        for m in range(members):
            for l in range(levels):
                out_ref[m * levels + l, pl.ds(t * SUB, SUB), :] = done[
                    l * SUB : (l + 1) * SUB, m * ny : (m + 1) * ny
                ]


def final_kernel(blocks, total_members, first, p_ref, base_ref, right_ref, fix_ref, lift_ref, *refs):
    got, out_ref = refs[:-1], refs[-1]
    members, levels, nx, ny = p_ref.shape
    place = lax.axis_index("gy")
    left = jnp.zeros(got[0].shape, F32)
    right = right_ref[...]
    for d in range(1, blocks):
        value = got[d - 1][...]
        left = left + jnp.where(place >= d, value, 0.0)
        right = right + jnp.where(place >= d, 0.0, value)
    enter = jnp.concatenate([left, right], 1)
    fix = fix_ref[...]
    share = 1.0 / (total_members - 1)
    for l in range(first, first + out_ref.shape[0]):
        high, low = split(enter * lift_ref[pl.ds(l, 1), :])
        add = dot(jnp.concatenate([high, high, low], 1), fix)
        out = jnp.zeros((nx, ny), F32)
        for m in range(members):
            out = out + p_ref[m, l].astype(F32) * (
                base_ref[m * levels + l] + add[m * nx : (m + 1) * nx]
            )
        out_ref[l - first] = out * share


def call(kernel, out, ins, scratch=(), far=False, flops=0):
    spec = lambda: pl.BlockSpec(memory_space=pltpu.HBM if far else VMEM)
    nbytes = sum(a.size * a.dtype.itemsize for a in ins) + sum(
        a.size * a.dtype.itemsize for a in jax.tree.leaves(out)
    )
    return pl.pallas_call(
        kernel,
        out_shape=out,
        in_specs=[spec() for _ in range(len(ins))],
        out_specs=jax.tree.map(lambda _: pl.BlockSpec(memory_space=VMEM), out),
        scratch_shapes=list(scratch),
        cost_estimate=pl.CostEstimate(flops=flops, bytes_accessed=nbytes, transcendentals=0),
        compiler_params=pltpu.CompilerParams(vmem_limit_bytes=GRANT),
    )(*ins)


def shape(*dims):
    return jax.ShapeDtypeStruct(dims, F32)


def exchange(values, axis, to):
    n = lax.axis_size(axis)
    got = []
    for d in range(1, n):
        got.append(lax.ppermute(values[d - 1], axis, [(i, to(i, d, n)) for i in range(n)]))
    return got


def body(perturb, gradient, vertical_eigenmodes, rate_x, rate_y):
    members, levels, nx, ny = perturb.shape
    modes = vertical_eigenmodes.shape[1]
    rows = members * modes
    blocks_x, blocks_y = lax.axis_size("gx"), lax.axis_size("gy")
    extent_x, extent_y = nx * blocks_x, ny * blocks_y

    field = shape(rows * nx, ny)
    pitch = (nx // SUB | 1) * SUB
    proj, alone, ends, hat, eigen, row_x, row_y, *messages = call(
        functools.partial(project_kernel, blocks_x, extent_x),
        tuple(
            [field, field, shape(ORDER * rows, ny), shape(rows, LANES)]
            + [shape(levels, modes), shape(1, modes), shape(1, modes)]
            + [shape(ORDER * rows, ny)] * (blocks_x - 1)
        ),
        tuple(
            pltpu.with_memory_space_constraint(a, pltpu.HBM)
            for a in (perturb, gradient, vertical_eigenmodes, rate_x[None, :], rate_y[None, :])
        ),
        scratch=(
            VMEM(perturb.shape, perturb.dtype),
            VMEM(gradient.shape, F32),
            VMEM((modes * SUB, 3 * levels * SUB), BF16),
            VMEM((rows * pitch, ny), F32),
            VMEM((rows * nx, ny), F32),
            pltpu.SemaphoreType.DMA((5,)),
        ),
        far=True,
        flops=1 << 28,
    )
    got = exchange(messages, "gx", target)
    packed = -(-(blocks_y - 1) * modes * ORDER // LANES) * LANES
    half = jax.ShapeDtypeStruct((modes, ny, ny), BF16)
    send, high, low, fix, lift, own = call(
        functools.partial(table_kernel, blocks_y, extent_y, extent_x),
        (
            shape(ny, packed),
            half,
            half,
            jax.ShapeDtypeStruct((6 * LANES, ny), BF16),
            shape(levels, 2 * LANES),
            shape(LANES, LANES),
        ),
        (eigen, row_x, row_y),
        flops=1 << 30,
    )
    before, react = call(
        functools.partial(early_kernel, extent_x),
        (shape(members * nx, packed), shape(2 * ORDER * nx, packed)),
        (alone, send, row_x),
        scratch=(
            VMEM((rows * nx, ny), F32),
            VMEM((SUB * nx, packed), F32),
            VMEM((packed // LANES, SUB * nx, LANES), F32),
        ),
        flops=1 << 29,
    )
    enter, *sent = call(
        functools.partial(x_kernel, blocks_x, blocks_y, extent_x),
        tuple([shape(2 * ORDER * rows, ny)] + [shape(members * nx, LANES)] * (blocks_y - 1)),
        (ends, hat, row_x, send, before, react, *got),
        flops=1 << 27,
    )
    got = exchange(sent, "gy", lambda i, d, n: (i + d) % n)
    base, right = call(
        functools.partial(local_kernel, extent_y, extent_x),
        (shape(members * levels, nx, ny), shape(members * nx, LANES)),
        (proj, enter, high, low, eigen, row_x, row_y, sent[0], own),
        scratch=(VMEM((rows * nx, ny), F32),) * 3,
        flops=1 << 29,
    )
    pieces = 4 if levels % 4 == 0 else 1
    size = levels // pieces
    parts = [
        call(
            functools.partial(final_kernel, blocks_y, members * lax.axis_size("member"), i * size),
            shape(size, nx, ny),
            (perturb, base, right, fix, lift, *got),
            flops=1 << 27,
        )
        for i in range(pieces)
    ]
    if lax.axis_size("member") > 2:
        return lax.psum(jnp.concatenate(parts, 0), "member")
    others = [lax.ppermute(part, "member", [(0, 1), (1, 0)]) for part in parts]
    return jnp.concatenate([a + b for a, b in zip(parts, others)], 0)


def solution(mesh):
    return jax.shard_map(
        body,
        mesh=mesh,
        in_specs=(P("member", None, "gx", "gy"), P(None, "gx", "gy"), P(), P(), P()),
        out_specs=P(None, "gx", "gy"),
        check_vma=False,
    )
```
